256 devices in a mesh: row: 16 (over y, x_lo, core), col: 16 (over x_hi, z).
Axes of the slice: x: 4 (x_hi: 2, x_lo: 2; x = x_hi * 2 + x_lo), y: 4, z: 8, core: 2. Of those that a mesh axis runs over, the one named last changes fastest.
Arguments:
- frames: bfloat16 [2, 64, 128, 2048], P(None, None, 'row', 'col'), may hold values from -6 to 6
- state: bfloat16 [64, 128, 2048], P(None, 'row', 'col'), may hold values from -1 to 1
- input_weight: bfloat16 [9, 192, 64], replicated, may hold values from -0.25 to 0.25
- state_weight: bfloat16 [9, 192, 64], replicated, may hold values from -0.25 to 0.25
- cotangent: bfloat16 [64, 128, 2048], P(None, 'row', 'col'), may hold values from -6 to 6
Outputs:
- final_state: bfloat16 [64, 128, 2048], P(None, 'row', 'col')
- grad_state: float32 [64, 128, 2048], P(None, 'row', 'col')
- grad_input_weights: float32 [9, 192, 64], replicated
- grad_state_weights: float32 [9, 192, 64], replicated
The draws below stay inside these ranges and needn't reach their ends.
All inputs are finite; a program needn't handle non-finite values.
Results may differ from the reference program's by a relative error of at most 0.0048.
Values may be sent and summed in bfloat16 or wider, within the bound.
A program may use at most 64 MiB of HBM per device.

```python
import jax
import jax.numpy as jnp
from jax import lax

C = 64
CI = 64
STEPS = 2
NY = 128
NX = 2048


def levels(rng, dims, cuts, smallest, high):
    factor_of, own = 1.0, jax.random.fold_in(rng, 6)
    for dim, blocks in cuts:
        heights = jnp.exp(jax.random.uniform(jax.random.fold_in(own, dim), (blocks,), jnp.float32, smallest / len(cuts), high / len(cuts)))
        factor_of = factor_of * jnp.repeat(heights, dims[dim] // blocks).reshape([-1 if axis == dim else 1 for axis in range(len(dims))])
    return factor_of


def noise(rng, dims, scale, most, split=(), dtype=jnp.bfloat16):
    level = levels(rng, dims, split, -0.22, 0.18) if split else 1.0
    result = jax.random.normal(rng, dims, jnp.float32) * scale * level
    return jnp.minimum(jnp.maximum(result, -most), most).astype(dtype)


def setup_inputs(seed: int = 0) -> dict:
    key_list = jax.random.split(jax.random.key(seed), 6)
    return {
        "frames": noise(key_list[0], (STEPS, CI, NY, NX), 1.0, 6.0, ((2, 16), (3, 16))),
        "state": jnp.clip(jax.random.uniform(key_list[1], (C, NY, NX), jnp.float32, -1.0, 1.0) * levels(key_list[1], (C, NY, NX), ((1, 16), (2, 16)), -0.4, 0.0), -1.0, 1.0).astype(jnp.bfloat16),
        "input_weight": noise(key_list[2], (9, 3 * C, CI), (9 * CI) ** -0.5, 0.25),
        "state_weight": noise(key_list[3], (9, 3 * C, C), (9 * C) ** -0.5, 0.25),
        "cotangent": noise(key_list[4], (C, NY, NX), 1.0, 6.0, ((1, 16), (2, 16))),
    }


def conv_taps(weights, padded, out_rows, out_cols):
    running = None
    for tap_index in range(9):
        window = padded[:, tap_index // 3:tap_index // 3 + out_rows, tap_index % 3:tap_index % 3 + out_cols]
        flattened = window.reshape(window.shape[0], out_rows * out_cols)
        product = jnp.dot(weights[tap_index], flattened, preferred_element_type=jnp.float32)
        running = product if running is None else running + product
    return running.reshape(weights.shape[1], out_rows, out_cols)

def gate_fields(frame_pad, state_pad, input_weight, state_weight, out_rows, out_cols):
    channels = state_weight.shape[2]
    from_input = conv_taps(input_weight, frame_pad, out_rows, out_cols)
    from_state = conv_taps(state_weight, state_pad, out_rows, out_cols)
    previous = state_pad[:, 1:-1, 1:-1].astype(jnp.float32)
    update = jax.nn.sigmoid(from_input[:channels] + from_state[:channels])
    reset_gate = jax.nn.sigmoid(from_input[channels:2 * channels] + from_state[channels:2 * channels])
    state_term = from_state[2 * channels:]
    candidate = jnp.tanh(from_input[2 * channels:] + reset_gate * state_term)
    new_state = ((1.0 - update) * candidate + update * previous).astype(jnp.bfloat16)
    return (new_state, (update, reset_gate, candidate, state_term))

def gate_grads(grad_state, saved, previous):
    update, reset_gate, candidate, state_term = saved
    grad_candidate = grad_state * (1.0 - update)
    grad_update = grad_state * (previous.astype(jnp.float32) - candidate)
    pre_update = grad_update * update * (1.0 - update)
    pre_candidate = grad_candidate * (1.0 - candidate * candidate)
    pre_reset = pre_candidate * state_term * reset_gate * (1.0 - reset_gate)
    pre_hidden = pre_candidate * reset_gate
    input_pre = jnp.concatenate([pre_update, pre_reset, pre_candidate], 0).astype(jnp.bfloat16)
    state_pre = jnp.concatenate([pre_update, pre_reset, pre_hidden], 0).astype(jnp.bfloat16)
    return (input_pre, state_pre, grad_state * update)

def weight_grad(pre_grad, padded, out_rows, out_cols):
    flat_pre = pre_grad.reshape(pre_grad.shape[0], out_rows * out_cols)
    pieces = []
    for tap_index in range(9):
        window = padded[:, tap_index // 3:tap_index // 3 + out_rows, tap_index % 3:tap_index % 3 + out_cols]
        flattened = window.reshape(window.shape[0], out_rows * out_cols)
        pieces.append(lax.dot_general(flat_pre, flattened, (((1,), (1,)), ((), ())), preferred_element_type=jnp.float32))
    return jnp.stack(pieces, 0)

def spread_back(weights, pre_grad, out_rows, out_cols):
    flat_pre = pre_grad.reshape(pre_grad.shape[0], out_rows * out_cols)
    padded = jnp.zeros((weights.shape[2], out_rows + 2, out_cols + 2), jnp.float32)
    for tap_index in range(9):
        product = lax.dot_general(weights[tap_index], flat_pre, (((0,), (0,)), ((), ())), preferred_element_type=jnp.float32)
        start_row = tap_index // 3
        start_col = tap_index % 3
        padded = padded.at[:, start_row:start_row + out_rows, start_col:start_col + out_cols].add(product.reshape(weights.shape[2], out_rows, out_cols))
    return padded

def pad_field(field_value):
    return jnp.pad(field_value, ((0, 0), (1, 1), (1, 1)))

def reference(frames, state, input_weight, state_weight, cotangent):
    step_count = frames.shape[0]
    rows = state.shape[1]
    cols = state.shape[2]
    records = []
    current = state
    for step_index in range(step_count):
        frame_pad = pad_field(frames[step_index])
        state_pad = pad_field(current)
        new_state, saved = gate_fields(frame_pad, state_pad, input_weight, state_weight, rows, cols)
        records.append((frame_pad, state_pad, saved))
        current = new_state
    grad_state = cotangent.astype(jnp.float32)
    input_sum = jnp.zeros(input_weight.shape, jnp.float32)
    state_sum = jnp.zeros(state_weight.shape, jnp.float32)
    for step_index in reversed(range(step_count)):
        frame_pad, state_pad, saved = records[step_index]
        input_pre, state_pre, direct = gate_grads(grad_state, saved, state_pad[:, 1:-1, 1:-1])
        input_sum = input_sum + weight_grad(input_pre, frame_pad, rows, cols)
        state_sum = state_sum + weight_grad(state_pre, state_pad, rows, cols)
        spread = spread_back(state_weight, state_pre, rows, cols)[:, 1:-1, 1:-1]
        grad_state = direct + spread
    loss_scale = (rows * cols) ** (-0.5)
    return (current, grad_state, input_sum * loss_scale, state_sum * loss_scale)
```

```python
import jax
import jax.numpy as jnp
from jax import lax
from jax.sharding import PartitionSpec as P


def padded_2(array, sides, width):
    for axis, dim in sides:
        devices, length = (lax.axis_size(axis), array.shape[dim])
        up = [(i, (i + 1) % devices) for i in range(devices - 1)]
        down = [(j, i) for i, j in up]
        last = lax.slice_in_dim(array, length - width, length, axis=dim)
        first = lax.slice_in_dim(array, 0, width, axis=dim)
        before = lax.ppermute(last, axis, up)
        after = lax.ppermute(first, axis, down)
        array = jnp.concatenate([before, array, after], axis=dim)
    return array


def conv_taps(weights, padded, out_rows, out_cols):
    running = None
    for tap_index in range(9):
        window = padded[
            :, tap_index // 3 : tap_index // 3 + out_rows, tap_index % 3 : tap_index % 3 + out_cols
        ]
        flattened = window.reshape(window.shape[0], out_rows * out_cols)
        product = jnp.dot(weights[tap_index], flattened, preferred_element_type=jnp.float32)
        running = product if running is None else running + product
    return running.reshape(weights.shape[1], out_rows, out_cols)


def gate_fields(frame_pad, state_pad, input_weight, state_weight, out_rows, out_cols):
    channels = state_weight.shape[2]
    from_input = conv_taps(input_weight, frame_pad, out_rows, out_cols)
    from_state = conv_taps(state_weight, state_pad, out_rows, out_cols)
    previous = state_pad[:, 1:-1, 1:-1].astype(jnp.float32)
    update = jax.nn.sigmoid(from_input[:channels] + from_state[:channels])
    reset_gate = jax.nn.sigmoid(
        from_input[channels : 2 * channels] + from_state[channels : 2 * channels]
    )
    state_term = from_state[2 * channels :]
    candidate = jnp.tanh(from_input[2 * channels :] + reset_gate * state_term)
    new_state = ((1.0 - update) * candidate + update * previous).astype(jnp.bfloat16)
    return (new_state, (update, reset_gate, candidate, state_term))


def gate_grads(grad_state, saved, previous):
    update, reset_gate, candidate, state_term = saved
    grad_candidate = grad_state * (1.0 - update)
    grad_update = grad_state * (previous.astype(jnp.float32) - candidate)
    pre_update = grad_update * update * (1.0 - update)
    pre_candidate = grad_candidate * (1.0 - candidate * candidate)
    pre_reset = pre_candidate * state_term * reset_gate * (1.0 - reset_gate)
    pre_hidden = pre_candidate * reset_gate
    input_pre = jnp.concatenate([pre_update, pre_reset, pre_candidate], 0).astype(jnp.bfloat16)
    state_pre = jnp.concatenate([pre_update, pre_reset, pre_hidden], 0).astype(jnp.bfloat16)
    return (input_pre, state_pre, grad_state * update)


def weight_grad(pre_grad, padded, out_rows, out_cols):
    flat_pre = pre_grad.reshape(pre_grad.shape[0], out_rows * out_cols)
    pieces = []
    for tap_index in range(9):
        window = padded[
            :, tap_index // 3 : tap_index // 3 + out_rows, tap_index % 3 : tap_index % 3 + out_cols
        ]
        flattened = window.reshape(window.shape[0], out_rows * out_cols)
        pieces.append(
            lax.dot_general(
                flat_pre, flattened, (((1,), (1,)), ((), ())), preferred_element_type=jnp.float32
            )
        )
    return jnp.stack(pieces, 0)


def spread_back(weights, pre_grad, out_rows, out_cols):
    flat_pre = pre_grad.reshape(pre_grad.shape[0], out_rows * out_cols)
    padded = jnp.zeros((weights.shape[2], out_rows + 2, out_cols + 2), jnp.float32)
    for tap_index in range(9):
        product = lax.dot_general(
            weights[tap_index],
            flat_pre,
            (((0,), (0,)), ((), ())),
            preferred_element_type=jnp.float32,
        )
        start_row = tap_index // 3
        start_col = tap_index % 3
        padded = padded.at[
            :, start_row : start_row + out_rows, start_col : start_col + out_cols
        ].add(product.reshape(weights.shape[2], out_rows, out_cols))
    return padded


def return_borders(padded):
    side_cols = jnp.stack([padded[:, :, 0], padded[:, :, -1]], 1)
    got_cols = padded_2(side_cols, (("col", 1),), 1)
    inner = padded[:, :, 1:-1]
    inner = inner.at[:, :, 0].add(got_cols[:, 0]).at[:, :, -1].add(got_cols[:, 3])
    side_rows = jnp.stack([inner[:, 0], inner[:, -1]], 1)
    got_rows = padded_2(side_rows.astype(jnp.bfloat16), (("row", 1),), 1).astype(side_rows.dtype)
    core = inner[:, 1:-1]
    return core.at[:, 0].add(got_rows[:, 0]).at[:, -1].add(got_rows[:, 3])


def local(frames, state, input_weight, state_weight, cotangent):
    step_count = frames.shape[0]
    rows = state.shape[1]
    cols = state.shape[2]
    records = []
    current = state
    for step_index in range(step_count):
        frame_pad, state_pad = (
            padded_2(frames[step_index], (("row", 1), ("col", 2)), 1),
            padded_2(current, (("row", 1), ("col", 2)), 1),
        )
        new_state, saved = gate_fields(frame_pad, state_pad, input_weight, state_weight, rows, cols)
        records.append((frame_pad, state_pad, saved))
        current = new_state
    grad_state = cotangent.astype(jnp.float32)
    input_sum = jnp.zeros(input_weight.shape, jnp.float32)
    state_sum = jnp.zeros(state_weight.shape, jnp.float32)
    for step_index in reversed(range(step_count)):
        frame_pad, state_pad, saved = records[step_index]
        input_pre, state_pre, direct = gate_grads(grad_state, saved, state_pad[:, 1:-1, 1:-1])
        input_share = weight_grad(input_pre, frame_pad, rows, cols)
        state_share = weight_grad(state_pre, state_pad, rows, cols)
        input_sum = input_sum + input_share
        state_sum = state_sum + state_share
        spread = return_borders(spread_back(state_weight, state_pre, rows, cols))
        grad_state = direct + spread
    both = jnp.stack([input_sum, state_sum], 0).reshape(256, -1)
    got = lax.all_to_all(both, ("row", "col"), 0, 0, tiled=True)
    part = jnp.sum(got, 0, keepdims=True)
    back = lax.all_to_all(jnp.broadcast_to(part, both.shape), ("row", "col"), 0, 0, tiled=True)
    both = back.reshape(2, 9, 192, 64)
    input_sum, state_sum = both[0], both[1]
    loss_scale = (rows * lax.axis_size("row") * cols * lax.axis_size("col")) ** (-0.5)
    return (current, grad_state, input_sum * loss_scale, state_sum * loss_scale)


def solution(mesh):
    in_specs = (P(None, None, "row", "col"), P(None, "row", "col"), P(), P(), P(None, "row", "col"))
    out_specs = (P(None, "row", "col"), P(None, "row", "col"), P(), P())
    return jax.shard_map(local, mesh=mesh, in_specs=in_specs, out_specs=out_specs, check_vma=False)
```

```python
import jax
import jax.numpy as jnp
from jax import lax
from jax.sharding import PartitionSpec as P

HALO = 4


def padded_2(array, sides, width):
    for axis, dim in sides:
        devices, length = (lax.axis_size(axis), array.shape[dim])
        up = [(i, (i + 1) % devices) for i in range(devices - 1)]
        down = [(j, i) for i, j in up]
        last = lax.slice_in_dim(array, length - width, length, axis=dim)
        first = lax.slice_in_dim(array, 0, width, axis=dim)
        before = lax.ppermute(last, axis, up)
        after = lax.ppermute(first, axis, down)
        array = jnp.concatenate([before, array, after], axis=dim)
    return array


def shifted(flat, offsets, margin, length):
    return jnp.concatenate([flat[:, margin + off : margin + off + length] for off in offsets], 0)


def conv_flat(weights, flat, offsets, margin, length):
    taps, out_ch, in_ch = weights.shape
    stack = shifted(flat, offsets, margin, length)
    matrix = weights.transpose(1, 0, 2).reshape(out_ch, taps * in_ch)
    return jnp.dot(matrix, stack, preferred_element_type=jnp.float32)


def spread_flat(weights, flat, offsets, margin, length):
    taps, out_ch, in_ch = weights.shape
    stack = shifted(flat, [-off for off in offsets], margin, length)
    matrix = weights.transpose(2, 0, 1).reshape(in_ch, taps * out_ch)
    return jnp.dot(matrix, stack, preferred_element_type=jnp.float32)


def weight_flat(pre_grad, flat, offsets, margin, length):
    taps = len(offsets)
    stack = shifted(flat, offsets, margin, length)
    share = lax.dot_general(
        pre_grad, stack, (((1,), (1,)), ((), ())), preferred_element_type=jnp.float32
    )
    return share.reshape(pre_grad.shape[0], taps, -1).transpose(1, 0, 2)


def gates(from_input, from_state, previous, channels):
    update = jax.nn.sigmoid(from_input[:channels] + from_state[:channels])
    reset_gate = jax.nn.sigmoid(
        from_input[channels : 2 * channels] + from_state[channels : 2 * channels]
    )
    state_term = from_state[2 * channels :]
    candidate = jnp.tanh(from_input[2 * channels :] + reset_gate * state_term)
    new_state = ((1.0 - update) * candidate + update * previous.astype(jnp.float32)).astype(
        jnp.bfloat16
    )
    return new_state, (update, reset_gate, candidate, state_term)


def gate_grads(grad_state, saved, previous):
    update, reset_gate, candidate, state_term = saved
    grad_candidate = grad_state * (1.0 - update)
    grad_update = grad_state * (previous.astype(jnp.float32) - candidate)
    pre_update = grad_update * update * (1.0 - update)
    pre_candidate = grad_candidate * (1.0 - candidate * candidate)
    pre_reset = pre_candidate * state_term * reset_gate * (1.0 - reset_gate)
    pre_hidden = pre_candidate * reset_gate
    input_pre = jnp.concatenate([pre_update, pre_reset, pre_candidate], 0).astype(jnp.bfloat16)
    state_pre = jnp.concatenate([pre_update, pre_reset, pre_hidden], 0).astype(jnp.bfloat16)
    return (input_pre, state_pre, grad_state * update)


def all_sum(parts):
    devices = lax.axis_size("row") * lax.axis_size("col")
    both = jnp.stack(parts, 0)
    flat = both.reshape(devices, -1)
    got = lax.all_to_all(flat, ("row", "col"), 0, 0, tiled=True)
    mine = jnp.sum(got, 0, keepdims=True)
    back = lax.all_to_all(jnp.broadcast_to(mine, flat.shape), ("row", "col"), 0, 0, tiled=True)
    return back.reshape(both.shape)


def local(frames, state, input_weight, state_weight, cotangent):
    step_count = frames.shape[0]
    channels = state.shape[0]
    rows, cols = state.shape[1], state.shape[2]
    halo = HALO
    ext_rows, ext_cols = rows + 2 * halo, cols + 2 * halo
    length = ext_rows * ext_cols
    margin = ext_cols + 1
    offsets = [(k // 3 - 1) * ext_cols + (k % 3 - 1) for k in range(9)]

    fields = jnp.concatenate([frames.reshape(-1, rows, cols), state, cotangent], 0)
    fields = padded_2(fields, (("row", 1), ("col", 2)), halo).reshape(-1, length)
    frame_flat = [fields[t * frames.shape[1] : (t + 1) * frames.shape[1]] for t in range(step_count)]
    base = step_count * frames.shape[1]
    state_flat = fields[base : base + channels]
    cot_flat = fields[base + channels :]

    r = lax.broadcasted_iota(jnp.int32, (ext_rows, ext_cols), 0)
    c = lax.broadcasted_iota(jnp.int32, (ext_rows, ext_cols), 1)
    global_r = lax.axis_index("row") * rows + r - halo
    global_c = lax.axis_index("col") * cols + c - halo
    inside = (
        (global_r >= 0)
        & (global_r < rows * lax.axis_size("row"))
        & (global_c >= 0)
        & (global_c < cols * lax.axis_size("col"))
    ).reshape(1, length)
    own = ((r >= halo) & (r < halo + rows) & (c >= halo) & (c < halo + cols)).reshape(1, length)

    def pad(flat):
        return jnp.pad(flat, ((0, 0), (margin, margin)))

    records = []
    current = state_flat
    for step_index in range(step_count):
        frame_pad, state_pad = pad(frame_flat[step_index]), pad(current)
        from_input = conv_flat(input_weight, frame_pad, offsets, margin, length)
        from_state = conv_flat(state_weight, state_pad, offsets, margin, length)
        new_state, saved = gates(from_input, from_state, current, channels)
        records.append((frame_pad, state_pad, current, saved))
        current = jnp.where(inside, new_state, jnp.zeros_like(new_state))

    grad_state = cot_flat.astype(jnp.float32)
    input_pres, input_fields, state_pres, state_fields = [], [], [], []
    for step_index in reversed(range(step_count)):
        frame_pad, state_pad, previous, saved = records[step_index]
        input_pre, state_pre, direct = gate_grads(grad_state, saved, previous)
        input_pres.append(jnp.where(own, input_pre, jnp.zeros_like(input_pre)))
        state_pres.append(jnp.where(own, state_pre, jnp.zeros_like(state_pre)))
        input_fields.append(frame_pad)
        state_fields.append(state_pad)
        state_pre = jnp.where(inside, state_pre, jnp.zeros_like(state_pre))
        grad_state = direct + spread_flat(state_weight, pad(state_pre), offsets, margin, length)

    input_sum = sum(
        weight_flat(p, f, offsets, margin, length) for p, f in zip(input_pres, input_fields)
    )
    state_sum = sum(
        weight_flat(p, f, offsets, margin, length) for p, f in zip(state_pres, state_fields)
    )
    input_sum, state_sum = all_sum([input_sum, state_sum])
    loss_scale = (rows * lax.axis_size("row") * cols * lax.axis_size("col")) ** (-0.5)

    def crop(flat):
        return flat.reshape(-1, ext_rows, ext_cols)[:, halo : halo + rows, halo : halo + cols]

    return (crop(current), crop(grad_state), input_sum * loss_scale, state_sum * loss_scale)


def solution(mesh):
    in_specs = (P(None, None, "row", "col"), P(None, "row", "col"), P(), P(), P(None, "row", "col"))
    out_specs = (P(None, "row", "col"), P(None, "row", "col"), P(), P())
    return jax.shard_map(local, mesh=mesh, in_specs=in_specs, out_specs=out_specs, check_vma=False)
```

```python
import functools

import jax
import jax.numpy as jnp
from jax import lax
from jax.experimental import pallas as pl
from jax.experimental.pallas import tpu as pltpu
from jax.sharding import PartitionSpec as P

HALO = 4


def padded_2(array, sides, width):
    for axis, dim in sides:
        devices, length = (lax.axis_size(axis), array.shape[dim])
        up = [(i, (i + 1) % devices) for i in range(devices - 1)]
        down = [(j, i) for i, j in up]
        last = lax.slice_in_dim(array, length - width, length, axis=dim)
        first = lax.slice_in_dim(array, 0, width, axis=dim)
        before = lax.ppermute(last, axis, up)
        after = lax.ppermute(first, axis, down)
        array = jnp.concatenate([before, array, after], axis=dim)
    return array


def shifted(flat, offsets, margin, length):
    return jnp.concatenate([flat[:, margin + off : margin + off + length] for off in offsets], 0)


def conv_flat(weights, flat, offsets, margin, length):
    taps, out_ch, in_ch = weights.shape
    stack = shifted(flat, offsets, margin, length)
    matrix = weights.transpose(1, 0, 2).reshape(out_ch, taps * in_ch)
    return jnp.dot(matrix, stack, preferred_element_type=jnp.float32)


def spread_flat(weights, flat, offsets, margin, length):
    taps, out_ch, in_ch = weights.shape
    stack = shifted(flat, [-off for off in offsets], margin, length)
    matrix = weights.transpose(2, 0, 1).reshape(in_ch, taps * out_ch)
    return jnp.dot(matrix, stack, preferred_element_type=jnp.float32)


def weight_flat(pre_grad, flat, offsets, margin, length):
    taps = len(offsets)
    stack = shifted(flat, offsets, margin, length)
    share = lax.dot_general(
        pre_grad, stack, (((1,), (1,)), ((), ())), preferred_element_type=jnp.float32
    )
    return share.reshape(pre_grad.shape[0], taps, -1).transpose(1, 0, 2)


def gates(from_input, from_state, previous, channels):
    update = jax.nn.sigmoid(from_input[:channels] + from_state[:channels])
    reset_gate = jax.nn.sigmoid(
        from_input[channels : 2 * channels] + from_state[channels : 2 * channels]
    )
    state_term = from_state[2 * channels :]
    candidate = jnp.tanh(from_input[2 * channels :] + reset_gate * state_term)
    new_state = ((1.0 - update) * candidate + update * previous.astype(jnp.float32)).astype(
        jnp.bfloat16
    )
    return new_state, (update, reset_gate, candidate, state_term)


def gate_grads(grad_state, saved, previous):
    update, reset_gate, candidate, state_term = saved
    grad_candidate = grad_state * (1.0 - update)
    grad_update = grad_state * (previous.astype(jnp.float32) - candidate)
    pre_update = grad_update * update * (1.0 - update)
    pre_candidate = grad_candidate * (1.0 - candidate * candidate)
    pre_reset = pre_candidate * state_term * reset_gate * (1.0 - reset_gate)
    pre_hidden = pre_candidate * reset_gate
    input_pre = jnp.concatenate([pre_update, pre_reset, pre_candidate], 0).astype(jnp.bfloat16)
    state_pre = jnp.concatenate([pre_update, pre_reset, pre_hidden], 0).astype(jnp.bfloat16)
    return (input_pre, state_pre, grad_state * update)


def exchange_kernel(axis, count, gather, x_ref, y_ref, send_sem, recv_sem, local_sem):
    me = lax.axis_index(axis)
    mesh_ids = pl.DeviceIdType.MESH
    barrier = pltpu.get_barrier_semaphore()
    for distance in range(1, count):
        peer = lax.rem(me + distance, count)
        pl.semaphore_signal(barrier, inc=1, device_id={axis: peer}, device_id_type=mesh_ids)
    pl.semaphore_wait(barrier, count - 1)
    copies = []
    for distance in range(1, count):
        peer = lax.rem(me + distance, count)
        copy = pltpu.make_async_remote_copy(
            src_ref=x_ref.at[0] if gather else x_ref.at[peer],
            dst_ref=y_ref.at[me],
            send_sem=send_sem.at[distance],
            recv_sem=recv_sem.at[distance],
            device_id={axis: peer},
            device_id_type=mesh_ids,
        )
        copy.start()
        copies.append(copy)
    own = pltpu.make_async_copy(x_ref.at[0] if gather else x_ref.at[me], y_ref.at[me], local_sem)
    own.start()
    own.wait()
    for copy in copies:
        copy.wait()


def exchange(x, axis, gather, collective_id):
    count = lax.axis_size(axis)
    return pl.pallas_call(
        functools.partial(exchange_kernel, axis, count, gather),
        out_shape=jax.ShapeDtypeStruct((count,) + x.shape[1:], x.dtype),
        in_specs=[pl.BlockSpec(memory_space=pltpu.VMEM)],
        out_specs=pl.BlockSpec(memory_space=pltpu.VMEM),
        scratch_shapes=[
            pltpu.SemaphoreType.DMA((count,)),
            pltpu.SemaphoreType.DMA((count,)),
            pltpu.SemaphoreType.DMA,
        ],
        compiler_params=pltpu.CompilerParams(collective_id=collective_id, has_side_effects=True),
    )(x)


def slots(size):
    return (size // 128, 128) if size % 128 == 0 else (1, size)


def all_sum(parts):
    both = jnp.stack(parts, 0)
    rows, cols = lax.axis_size("row"), lax.axis_size("col")
    first = both.size // rows
    second = first // cols
    got = exchange(both.reshape((rows,) + slots(first)), "row", False, 0)
    mine = jnp.sum(got, 0).reshape((cols,) + slots(second))
    got = exchange(mine, "col", False, 1)
    mine = jnp.sum(got, 0, keepdims=True)
    got = exchange(mine, "col", True, 2).reshape((1,) + slots(first))
    got = exchange(got, "row", True, 3)
    return got.reshape(both.shape)


def local(frames, state, input_weight, state_weight, cotangent):
    step_count = frames.shape[0]
    channels = state.shape[0]
    rows, cols = state.shape[1], state.shape[2]
    halo = HALO
    ext_rows, ext_cols = rows + 2 * halo, cols + 2 * halo
    length = ext_rows * ext_cols
    margin = ext_cols + 1
    offsets = [(k // 3 - 1) * ext_cols + (k % 3 - 1) for k in range(9)]

    fields = jnp.concatenate([frames.reshape(-1, rows, cols), state, cotangent], 0)
    fields = padded_2(fields, (("row", 1), ("col", 2)), halo).reshape(-1, length)
    frame_flat = [fields[t * frames.shape[1] : (t + 1) * frames.shape[1]] for t in range(step_count)]
    base = step_count * frames.shape[1]
    state_flat = fields[base : base + channels]
    cot_flat = fields[base + channels :]

    r = lax.broadcasted_iota(jnp.int32, (ext_rows, ext_cols), 0)
    c = lax.broadcasted_iota(jnp.int32, (ext_rows, ext_cols), 1)
    global_r = lax.axis_index("row") * rows + r - halo
    global_c = lax.axis_index("col") * cols + c - halo
    inside = (
        (global_r >= 0)
        & (global_r < rows * lax.axis_size("row"))
        & (global_c >= 0)
        & (global_c < cols * lax.axis_size("col"))
    ).reshape(1, length)
    own = ((r >= halo) & (r < halo + rows) & (c >= halo) & (c < halo + cols)).reshape(1, length)

    def pad(flat):
        return jnp.pad(flat, ((0, 0), (margin, margin)))

    records = []
    current = state_flat
    for step_index in range(step_count):
        frame_pad, state_pad = pad(frame_flat[step_index]), pad(current)
        from_input = conv_flat(input_weight, frame_pad, offsets, margin, length)
        from_state = conv_flat(state_weight, state_pad, offsets, margin, length)
        new_state, saved = gates(from_input, from_state, current, channels)
        records.append((frame_pad, state_pad, current, saved))
        current = jnp.where(inside, new_state, jnp.zeros_like(new_state))

    grad_state = cot_flat.astype(jnp.float32)
    input_pres, input_fields, state_pres, state_fields = [], [], [], []
    for step_index in reversed(range(step_count)):
        frame_pad, state_pad, previous, saved = records[step_index]
        input_pre, state_pre, direct = gate_grads(grad_state, saved, previous)
        input_pres.append(jnp.where(own, input_pre, jnp.zeros_like(input_pre)))
        state_pres.append(jnp.where(own, state_pre, jnp.zeros_like(state_pre)))
        input_fields.append(frame_pad)
        state_fields.append(state_pad)
        state_pre = jnp.where(inside, state_pre, jnp.zeros_like(state_pre))
        grad_state = direct + spread_flat(state_weight, pad(state_pre), offsets, margin, length)

    input_sum = sum(
        weight_flat(p, f, offsets, margin, length) for p, f in zip(input_pres, input_fields)
    )
    state_sum = sum(
        weight_flat(p, f, offsets, margin, length) for p, f in zip(state_pres, state_fields)
    )
    input_sum, state_sum = all_sum([input_sum, state_sum])
    loss_scale = (rows * lax.axis_size("row") * cols * lax.axis_size("col")) ** (-0.5)

    def crop(flat):
        return flat.reshape(-1, ext_rows, ext_cols)[:, halo : halo + rows, halo : halo + cols]

    return (crop(current), crop(grad_state), input_sum * loss_scale, state_sum * loss_scale)


def solution(mesh):
    in_specs = (P(None, None, "row", "col"), P(None, "row", "col"), P(), P(), P(None, "row", "col"))
    out_specs = (P(None, "row", "col"), P(None, "row", "col"), P(), P())
    return jax.shard_map(local, mesh=mesh, in_specs=in_specs, out_specs=out_specs, check_vma=False)
```

```python
import functools

import jax
import jax.numpy as jnp
from jax import lax
from jax.experimental import pallas as pl
from jax.experimental.pallas import tpu as pltpu
from jax.sharding import PartitionSpec as P

HALO = 4


def padded_2(array, sides, width):
    for axis, dim in sides:
        devices, length = (lax.axis_size(axis), array.shape[dim])
        up = [(i, (i + 1) % devices) for i in range(devices - 1)]
        down = [(j, i) for i, j in up]
        last = lax.slice_in_dim(array, length - width, length, axis=dim)
        first = lax.slice_in_dim(array, 0, width, axis=dim)
        before = lax.ppermute(last, axis, up)
        after = lax.ppermute(first, axis, down)
        array = jnp.concatenate([before, array, after], axis=dim)
    return array


def shifted(flat, offsets, margin, length):
    return jnp.concatenate([flat[:, margin + off : margin + off + length] for off in offsets], 0)


def conv_flat(weights, flat, offsets, margin, length):
    taps, out_ch, in_ch = weights.shape
    stack = shifted(flat, offsets, margin, length)
    matrix = weights.transpose(1, 0, 2).reshape(out_ch, taps * in_ch)
    return jnp.dot(matrix, stack, preferred_element_type=jnp.float32)


def spread_flat(weights, flat, offsets, margin, length):
    taps, out_ch, in_ch = weights.shape
    stack = shifted(flat, [-off for off in offsets], margin, length)
    matrix = weights.transpose(2, 0, 1).reshape(in_ch, taps * out_ch)
    return jnp.dot(matrix, stack, preferred_element_type=jnp.float32)


def weight_flat(pre_grad, flat, offsets, margin, length):
    taps = len(offsets)
    stack = shifted(flat, offsets, margin, length)
    share = lax.dot_general(
        pre_grad, stack, (((1,), (1,)), ((), ())), preferred_element_type=jnp.float32
    )
    return share.reshape(pre_grad.shape[0], taps, -1).transpose(1, 0, 2)


def gates(from_input, from_state, previous, channels):
    update = jax.nn.sigmoid(from_input[:channels] + from_state[:channels])
    reset_gate = jax.nn.sigmoid(
        from_input[channels : 2 * channels] + from_state[channels : 2 * channels]
    )
    state_term = from_state[2 * channels :]
    candidate = jnp.tanh(from_input[2 * channels :] + reset_gate * state_term)
    new_state = ((1.0 - update) * candidate + update * previous.astype(jnp.float32)).astype(
        jnp.bfloat16
    )
    return new_state, (update, reset_gate, candidate, state_term)


def gate_grads(grad_state, saved, previous):
    update, reset_gate, candidate, state_term = saved
    grad_candidate = grad_state * (1.0 - update)
    grad_update = grad_state * (previous.astype(jnp.float32) - candidate)
    pre_update = grad_update * update * (1.0 - update)
    pre_candidate = grad_candidate * (1.0 - candidate * candidate)
    pre_reset = pre_candidate * state_term * reset_gate * (1.0 - reset_gate)
    pre_hidden = pre_candidate * reset_gate
    input_pre = jnp.concatenate([pre_update, pre_reset, pre_candidate], 0).astype(jnp.bfloat16)
    state_pre = jnp.concatenate([pre_update, pre_reset, pre_hidden], 0).astype(jnp.bfloat16)
    return (input_pre, state_pre, grad_state * update)


def reduce_kernel(rows, cols, x_ref, out_ref, got_row, summed, got_col, reduced, gathered, send_sem, recv_sem, own_sem):
    mesh_ids = pl.DeviceIdType.MESH
    me_row, me_col = lax.axis_index("row"), lax.axis_index("col")
    barrier = pltpu.get_barrier_semaphore()
    for axis, me, count in (("row", me_row, rows), ("col", me_col, cols)):
        for distance in range(1, count):
            peer = lax.rem(me + distance, count)
            pl.semaphore_signal(barrier, inc=1, device_id={axis: peer}, device_id_type=mesh_ids)
    pl.semaphore_wait(barrier, rows + cols - 2)
    piece = summed.shape[0] // cols

    def phase(index, axis, me, count, source, target):
        copies = []
        for distance in range(1, count):
            peer = lax.rem(me + distance, count)
            copy = pltpu.make_async_remote_copy(
                src_ref=source(peer),
                dst_ref=target.at[me],
                send_sem=send_sem.at[index, distance],
                recv_sem=recv_sem.at[index, distance],
                device_id={axis: peer},
                device_id_type=mesh_ids,
            )
            copy.start()
            copies.append(copy)
        own = pltpu.make_async_copy(source(me), target.at[me], own_sem.at[index])
        own.start()
        own.wait()
        for copy in copies:
            copy.wait()

    phase(0, "row", me_row, rows, lambda peer: x_ref.at[peer], got_row)
    total = got_row[0]
    for index in range(1, rows):
        total = total + got_row[index]
    summed[...] = total
    phase(
        1, "col", me_col, cols,
        lambda peer: summed.at[pl.ds(pl.multiple_of(peer * piece, piece), piece)], got_col,
    )
    total = got_col[0]
    for index in range(1, cols):
        total = total + got_col[index]
    reduced[...] = total
    phase(2, "col", me_col, cols, lambda peer: reduced, gathered)
    phase(3, "row", me_row, rows, lambda peer: gathered, out_ref)


def all_sum(parts):
    both = jnp.stack(parts, 0)
    rows, cols = lax.axis_size("row"), lax.axis_size("col")
    lanes = 128
    piece = -(-both.size // (rows * cols * lanes))
    piece = -(-piece // 8) * 8
    chunk = cols * piece * lanes
    padded_size = rows * chunk
    flat = jnp.pad(both.reshape(-1), (0, padded_size - both.size))
    count = max(rows, cols)
    out = pl.pallas_call(
        functools.partial(reduce_kernel, rows, cols),
        out_shape=jax.ShapeDtypeStruct((rows, cols, piece, lanes), jnp.float32),
        in_specs=[pl.BlockSpec(memory_space=pltpu.VMEM)],
        out_specs=pl.BlockSpec(memory_space=pltpu.VMEM),
        scratch_shapes=[
            pltpu.VMEM((rows, cols * piece, lanes), jnp.float32),
            pltpu.VMEM((cols * piece, lanes), jnp.float32),
            pltpu.VMEM((cols, piece, lanes), jnp.float32),
            pltpu.VMEM((piece, lanes), jnp.float32),
            pltpu.VMEM((cols, piece, lanes), jnp.float32),
            pltpu.SemaphoreType.DMA((4, count)),
            pltpu.SemaphoreType.DMA((4, count)),
            pltpu.SemaphoreType.DMA((4,)),
        ],
        compiler_params=pltpu.CompilerParams(collective_id=0, has_side_effects=True),
    )(flat.reshape(rows, cols * piece, lanes))
    return out.reshape(-1)[: both.size].reshape(both.shape)


def local(frames, state, input_weight, state_weight, cotangent):
    step_count = frames.shape[0]
    channels = state.shape[0]
    rows, cols = state.shape[1], state.shape[2]
    halo = HALO
    ext_rows, ext_cols = rows + 2 * halo, cols + 2 * halo
    length = ext_rows * ext_cols
    margin = ext_cols + 1
    offsets = [(k // 3 - 1) * ext_cols + (k % 3 - 1) for k in range(9)]

    fields = jnp.concatenate([frames.reshape(-1, rows, cols), state, cotangent], 0)
    fields = padded_2(fields, (("row", 1), ("col", 2)), halo).reshape(-1, length)
    frame_flat = [fields[t * frames.shape[1] : (t + 1) * frames.shape[1]] for t in range(step_count)]
    base = step_count * frames.shape[1]
    state_flat = fields[base : base + channels]
    cot_flat = fields[base + channels :]

    r = lax.broadcasted_iota(jnp.int32, (ext_rows, ext_cols), 0)
    c = lax.broadcasted_iota(jnp.int32, (ext_rows, ext_cols), 1)
    global_r = lax.axis_index("row") * rows + r - halo
    global_c = lax.axis_index("col") * cols + c - halo
    inside = (
        (global_r >= 0)
        & (global_r < rows * lax.axis_size("row"))
        & (global_c >= 0)
        & (global_c < cols * lax.axis_size("col"))
    ).reshape(1, length)
    own = ((r >= halo) & (r < halo + rows) & (c >= halo) & (c < halo + cols)).reshape(1, length)

    def pad(flat):
        return jnp.pad(flat, ((0, 0), (margin, margin)))

    records = []
    current = state_flat
    for step_index in range(step_count):
        frame_pad, state_pad = pad(frame_flat[step_index]), pad(current)
        from_input = conv_flat(input_weight, frame_pad, offsets, margin, length)
        from_state = conv_flat(state_weight, state_pad, offsets, margin, length)
        new_state, saved = gates(from_input, from_state, current, channels)
        records.append((frame_pad, state_pad, current, saved))
        current = jnp.where(inside, new_state, jnp.zeros_like(new_state))

    grad_state = cot_flat.astype(jnp.float32)
    input_pres, input_fields, state_pres, state_fields = [], [], [], []
    for step_index in reversed(range(step_count)):
        frame_pad, state_pad, previous, saved = records[step_index]
        input_pre, state_pre, direct = gate_grads(grad_state, saved, previous)
        input_pres.append(jnp.where(own, input_pre, jnp.zeros_like(input_pre)))
        state_pres.append(jnp.where(own, state_pre, jnp.zeros_like(state_pre)))
        input_fields.append(frame_pad)
        state_fields.append(state_pad)
        state_pre = jnp.where(inside, state_pre, jnp.zeros_like(state_pre))
        grad_state = direct + spread_flat(state_weight, pad(state_pre), offsets, margin, length)

    input_sum = sum(
        weight_flat(p, f, offsets, margin, length) for p, f in zip(input_pres, input_fields)
    )
    state_sum = sum(
        weight_flat(p, f, offsets, margin, length) for p, f in zip(state_pres, state_fields)
    )
    input_sum, state_sum = all_sum([input_sum, state_sum])
    loss_scale = (rows * lax.axis_size("row") * cols * lax.axis_size("col")) ** (-0.5)

    def crop(flat):
        return flat.reshape(-1, ext_rows, ext_cols)[:, halo : halo + rows, halo : halo + cols]

    return (crop(current), crop(grad_state), input_sum * loss_scale, state_sum * loss_scale)


def solution(mesh):
    in_specs = (P(None, None, "row", "col"), P(None, "row", "col"), P(), P(), P(None, "row", "col"))
    out_specs = (P(None, "row", "col"), P(None, "row", "col"), P(), P())
    return jax.shard_map(local, mesh=mesh, in_specs=in_specs, out_specs=out_specs, check_vma=False)
```

```python
import functools

import jax
import jax.numpy as jnp
from jax import lax
from jax.experimental import pallas as pl
from jax.experimental.pallas import tpu as pltpu
from jax.sharding import PartitionSpec as P

HALO = 4


def halo_all(array, width):
    rows, cols = lax.axis_size("row"), lax.axis_size("col")
    height, breadth = array.shape[1], array.shape[2]
    low_r, high_r = slice(0, width), slice(height - width, height)
    low_c, high_c = slice(0, width), slice(breadth - width, breadth)
    whole_r, whole_c = slice(0, height), slice(0, breadth)

    def fetch(down, right, rows_taken, cols_taken):
        pairs = [
            (r * cols + c, (r + down) * cols + c + right)
            for r in range(rows)
            for c in range(cols)
            if 0 <= r + down < rows and 0 <= c + right < cols
        ]
        return lax.ppermute(array[:, rows_taken, cols_taken], ("row", "col"), pairs)

    top = jnp.concatenate(
        [fetch(1, 1, high_r, high_c), fetch(1, 0, high_r, whole_c), fetch(1, -1, high_r, low_c)], 2
    )
    middle = jnp.concatenate([fetch(0, 1, whole_r, high_c), array, fetch(0, -1, whole_r, low_c)], 2)
    bottom = jnp.concatenate(
        [fetch(-1, 1, low_r, high_c), fetch(-1, 0, low_r, whole_c), fetch(-1, -1, low_r, low_c)], 2
    )
    return jnp.concatenate([top, middle, bottom], 1)


def shifted(flat, offsets, margin, length):
    return jnp.concatenate([flat[:, margin + off : margin + off + length] for off in offsets], 0)


def conv_flat(weights, flat, offsets, margin, length):
    taps, out_ch, in_ch = weights.shape
    stack = shifted(flat, offsets, margin, length)
    matrix = weights.transpose(1, 0, 2).reshape(out_ch, taps * in_ch)
    return jnp.dot(matrix, stack, preferred_element_type=jnp.float32)


def spread_flat(weights, flat, offsets, margin, length):
    taps, out_ch, in_ch = weights.shape
    stack = shifted(flat, [-off for off in offsets], margin, length)
    matrix = weights.transpose(2, 0, 1).reshape(in_ch, taps * out_ch)
    return jnp.dot(matrix, stack, preferred_element_type=jnp.float32)


def weight_flat(pre_grad, flat, offsets, margin, length):
    taps = len(offsets)
    stack = shifted(flat, offsets, margin, length)
    share = lax.dot_general(
        pre_grad, stack, (((1,), (1,)), ((), ())), preferred_element_type=jnp.float32
    )
    return share.reshape(pre_grad.shape[0], taps, -1).transpose(1, 0, 2)


def gates(from_input, from_state, previous, channels):
    update = jax.nn.sigmoid(from_input[:channels] + from_state[:channels])
    reset_gate = jax.nn.sigmoid(
        from_input[channels : 2 * channels] + from_state[channels : 2 * channels]
    )
    state_term = from_state[2 * channels :]
    candidate = jnp.tanh(from_input[2 * channels :] + reset_gate * state_term)
    new_state = ((1.0 - update) * candidate + update * previous.astype(jnp.float32)).astype(
        jnp.bfloat16
    )
    return new_state, (update, reset_gate, candidate, state_term)


def gate_grads(grad_state, saved, previous):
    update, reset_gate, candidate, state_term = saved
    grad_candidate = grad_state * (1.0 - update)
    grad_update = grad_state * (previous.astype(jnp.float32) - candidate)
    pre_update = grad_update * update * (1.0 - update)
    pre_candidate = grad_candidate * (1.0 - candidate * candidate)
    pre_reset = pre_candidate * state_term * reset_gate * (1.0 - reset_gate)
    pre_hidden = pre_candidate * reset_gate
    input_pre = jnp.concatenate([pre_update, pre_reset, pre_candidate], 0).astype(jnp.bfloat16)
    state_pre = jnp.concatenate([pre_update, pre_reset, pre_hidden], 0).astype(jnp.bfloat16)
    return (input_pre, state_pre, grad_state * update)


def reduce_kernel(rows, cols, x_ref, out_ref, got_row, summed, got_col, reduced, gathered, send_sem, recv_sem, own_sem):
    mesh_ids = pl.DeviceIdType.MESH
    me_row, me_col = lax.axis_index("row"), lax.axis_index("col")
    barrier = pltpu.get_barrier_semaphore()
    for axis, me, count in (("row", me_row, rows), ("col", me_col, cols)):
        for distance in range(1, count):
            peer = lax.rem(me + distance, count)
            pl.semaphore_signal(barrier, inc=1, device_id={axis: peer}, device_id_type=mesh_ids)
    pl.semaphore_wait(barrier, rows + cols - 2)
    piece = summed.shape[0] // cols

    def phase(index, axis, me, count, source, target):
        copies = []
        for distance in range(1, count):
            peer = lax.rem(me + distance, count)
            copy = pltpu.make_async_remote_copy(
                src_ref=source(peer),
                dst_ref=target.at[me],
                send_sem=send_sem.at[index, distance],
                recv_sem=recv_sem.at[index, distance],
                device_id={axis: peer},
                device_id_type=mesh_ids,
            )
            copy.start()
            copies.append(copy)
        own = pltpu.make_async_copy(source(me), target.at[me], own_sem.at[index])
        own.start()
        own.wait()
        for copy in copies:
            copy.wait()

    phase(0, "row", me_row, rows, lambda peer: x_ref.at[peer], got_row)
    total = got_row[0]
    for index in range(1, rows):
        total = total + got_row[index]
    summed[...] = total
    phase(
        1, "col", me_col, cols,
        lambda peer: summed.at[pl.ds(pl.multiple_of(peer * piece, piece), piece)], got_col,
    )
    total = got_col[0]
    for index in range(1, cols):
        total = total + got_col[index]
    reduced[...] = total
    phase(2, "col", me_col, cols, lambda peer: reduced, gathered)
    phase(3, "row", me_row, rows, lambda peer: gathered, out_ref)


def all_sum(parts):
    both = jnp.stack(parts, 0)
    rows, cols = lax.axis_size("row"), lax.axis_size("col")
    lanes = 128
    piece = -(-both.size // (rows * cols * lanes))
    piece = -(-piece // 8) * 8
    chunk = cols * piece * lanes
    padded_size = rows * chunk
    flat = jnp.pad(both.reshape(-1), (0, padded_size - both.size))
    count = max(rows, cols)
    out = pl.pallas_call(
        functools.partial(reduce_kernel, rows, cols),
        out_shape=jax.ShapeDtypeStruct((rows, cols, piece, lanes), jnp.float32),
        in_specs=[pl.BlockSpec(memory_space=pltpu.VMEM)],
        out_specs=pl.BlockSpec(memory_space=pltpu.VMEM),
        scratch_shapes=[
            pltpu.VMEM((rows, cols * piece, lanes), jnp.float32),
            pltpu.VMEM((cols * piece, lanes), jnp.float32),
            pltpu.VMEM((cols, piece, lanes), jnp.float32),
            pltpu.VMEM((piece, lanes), jnp.float32),
            pltpu.VMEM((cols, piece, lanes), jnp.float32),
            pltpu.SemaphoreType.DMA((4, count)),
            pltpu.SemaphoreType.DMA((4, count)),
            pltpu.SemaphoreType.DMA((4,)),
        ],
        compiler_params=pltpu.CompilerParams(collective_id=0, has_side_effects=True),
    )(flat.reshape(rows, cols * piece, lanes))
    return out.reshape(-1)[: both.size].reshape(both.shape)


def local(frames, state, input_weight, state_weight, cotangent):
    step_count = frames.shape[0]
    channels = state.shape[0]
    rows, cols = state.shape[1], state.shape[2]
    halo = HALO
    ext_rows, ext_cols = rows + 2 * halo, cols + 2 * halo
    length = ext_rows * ext_cols
    margin = ext_cols + 1
    offsets = [(k // 3 - 1) * ext_cols + (k % 3 - 1) for k in range(9)]

    fields = jnp.concatenate([frames.reshape(-1, rows, cols), state, cotangent], 0)
    fields = halo_all(fields, halo).reshape(-1, length)
    frame_flat = [fields[t * frames.shape[1] : (t + 1) * frames.shape[1]] for t in range(step_count)]
    base = step_count * frames.shape[1]
    state_flat = fields[base : base + channels]
    cot_flat = fields[base + channels :]

    r = lax.broadcasted_iota(jnp.int32, (ext_rows, ext_cols), 0)
    c = lax.broadcasted_iota(jnp.int32, (ext_rows, ext_cols), 1)
    global_r = lax.axis_index("row") * rows + r - halo
    global_c = lax.axis_index("col") * cols + c - halo
    inside = (
        (global_r >= 0)
        & (global_r < rows * lax.axis_size("row"))
        & (global_c >= 0)
        & (global_c < cols * lax.axis_size("col"))
    ).reshape(1, length)
    own = ((r >= halo) & (r < halo + rows) & (c >= halo) & (c < halo + cols)).reshape(1, length)

    def pad(flat):
        return jnp.pad(flat, ((0, 0), (margin, margin)))

    records = []
    current = state_flat
    for step_index in range(step_count):
        frame_pad, state_pad = pad(frame_flat[step_index]), pad(current)
        from_input = conv_flat(input_weight, frame_pad, offsets, margin, length)
        from_state = conv_flat(state_weight, state_pad, offsets, margin, length)
        new_state, saved = gates(from_input, from_state, current, channels)
        records.append((frame_pad, state_pad, current, saved))
        current = jnp.where(inside, new_state, jnp.zeros_like(new_state))

    grad_state = cot_flat.astype(jnp.float32)
    input_pres, input_fields, state_pres, state_fields = [], [], [], []
    for step_index in reversed(range(step_count)):
        frame_pad, state_pad, previous, saved = records[step_index]
        input_pre, state_pre, direct = gate_grads(grad_state, saved, previous)
        input_pres.append(jnp.where(own, input_pre, jnp.zeros_like(input_pre)))
        state_pres.append(jnp.where(own, state_pre, jnp.zeros_like(state_pre)))
        input_fields.append(frame_pad)
        state_fields.append(state_pad)
        state_pre = jnp.where(inside, state_pre, jnp.zeros_like(state_pre))
        grad_state = direct + spread_flat(state_weight, pad(state_pre), offsets, margin, length)

    input_sum = sum(
        weight_flat(p, f, offsets, margin, length) for p, f in zip(input_pres, input_fields)
    )
    state_sum = sum(
        weight_flat(p, f, offsets, margin, length) for p, f in zip(state_pres, state_fields)
    )
    input_sum, state_sum = all_sum([input_sum, state_sum])
    loss_scale = (rows * lax.axis_size("row") * cols * lax.axis_size("col")) ** (-0.5)

    def crop(flat):
        return flat.reshape(-1, ext_rows, ext_cols)[:, halo : halo + rows, halo : halo + cols]

    return (crop(current), crop(grad_state), input_sum * loss_scale, state_sum * loss_scale)


def solution(mesh):
    in_specs = (P(None, None, "row", "col"), P(None, "row", "col"), P(), P(), P(None, "row", "col"))
    out_specs = (P(None, "row", "col"), P(None, "row", "col"), P(), P())
    return jax.shard_map(local, mesh=mesh, in_specs=in_specs, out_specs=out_specs, check_vma=False)
```

```python
import functools

import jax
import jax.numpy as jnp
from jax import lax
from jax.experimental import pallas as pl
from jax.experimental.pallas import tpu as pltpu
from jax.sharding import PartitionSpec as P

HALO = 4


def padded_2(array, sides, width):
    for axis, dim in sides:
        devices, length = (lax.axis_size(axis), array.shape[dim])
        up = [(i, (i + 1) % devices) for i in range(devices - 1)]
        down = [(j, i) for i, j in up]
        last = lax.slice_in_dim(array, length - width, length, axis=dim)
        first = lax.slice_in_dim(array, 0, width, axis=dim)
        before = lax.ppermute(last, axis, up)
        after = lax.ppermute(first, axis, down)
        array = jnp.concatenate([before, array, after], axis=dim)
    return array


def shifted(field, field_start, out_start, length, offsets):
    base = out_start - field_start
    return jnp.concatenate([field[:, base + off : base + off + length] for off in offsets], 0)


def conv_flat(weights, field, field_start, span, offsets):
    taps, out_ch, in_ch = weights.shape
    stack = shifted(field, field_start, span[0], span[1] - span[0], offsets)
    matrix = weights.transpose(1, 0, 2).reshape(out_ch, taps * in_ch)
    return jnp.dot(matrix, stack, preferred_element_type=jnp.float32)


def spread_flat(weights, field, field_start, span, offsets):
    taps, out_ch, in_ch = weights.shape
    stack = shifted(field, field_start, span[0], span[1] - span[0], [-off for off in offsets])
    matrix = weights.transpose(2, 0, 1).reshape(in_ch, taps * out_ch)
    return jnp.dot(matrix, stack, preferred_element_type=jnp.float32)


def weight_flat(pre_grad, field, field_start, span, offsets):
    taps = len(offsets)
    stack = shifted(field, field_start, span[0], span[1] - span[0], offsets)
    share = lax.dot_general(
        pre_grad, stack, (((1,), (1,)), ((), ())), preferred_element_type=jnp.float32
    )
    return share.reshape(pre_grad.shape[0], taps, -1).transpose(1, 0, 2)


def cut(field, field_start, span):
    return field[:, span[0] - field_start : span[1] - field_start]


def gates(from_input, from_state, previous, channels):
    update = jax.nn.sigmoid(from_input[:channels] + from_state[:channels])
    reset_gate = jax.nn.sigmoid(
        from_input[channels : 2 * channels] + from_state[channels : 2 * channels]
    )
    state_term = from_state[2 * channels :]
    candidate = jnp.tanh(from_input[2 * channels :] + reset_gate * state_term)
    new_state = ((1.0 - update) * candidate + update * previous.astype(jnp.float32)).astype(
        jnp.bfloat16
    )
    return new_state, (update, reset_gate, candidate, state_term)


def gate_grads(grad_state, saved, previous):
    update, reset_gate, candidate, state_term = saved
    grad_candidate = grad_state * (1.0 - update)
    grad_update = grad_state * (previous.astype(jnp.float32) - candidate)
    pre_update = grad_update * update * (1.0 - update)
    pre_candidate = grad_candidate * (1.0 - candidate * candidate)
    pre_reset = pre_candidate * state_term * reset_gate * (1.0 - reset_gate)
    pre_hidden = pre_candidate * reset_gate
    input_pre = jnp.concatenate([pre_update, pre_reset, pre_candidate], 0).astype(jnp.bfloat16)
    state_pre = jnp.concatenate([pre_update, pre_reset, pre_hidden], 0).astype(jnp.bfloat16)
    return (input_pre, state_pre, grad_state * update)


def reduce_kernel(rows, cols, x_ref, out_ref, got_row, summed, got_col, reduced, gathered, send_sem, recv_sem, own_sem):
    mesh_ids = pl.DeviceIdType.MESH
    me_row, me_col = lax.axis_index("row"), lax.axis_index("col")
    barrier = pltpu.get_barrier_semaphore()
    for axis, me, count in (("row", me_row, rows), ("col", me_col, cols)):
        for distance in range(1, count):
            peer = lax.rem(me + distance, count)
            pl.semaphore_signal(barrier, inc=1, device_id={axis: peer}, device_id_type=mesh_ids)
    pl.semaphore_wait(barrier, rows + cols - 2)
    piece = summed.shape[0] // cols

    def phase(index, axis, me, count, source, target):
        copies = []
        for distance in range(1, count):
            peer = lax.rem(me + distance, count)
            copy = pltpu.make_async_remote_copy(
                src_ref=source(peer),
                dst_ref=target.at[me],
                send_sem=send_sem.at[index, distance],
                recv_sem=recv_sem.at[index, distance],
                device_id={axis: peer},
                device_id_type=mesh_ids,
            )
            copy.start()
            copies.append(copy)
        own = pltpu.make_async_copy(source(me), target.at[me], own_sem.at[index])
        own.start()
        own.wait()
        for copy in copies:
            copy.wait()

    phase(0, "row", me_row, rows, lambda peer: x_ref.at[peer], got_row)
    total = got_row[0]
    for index in range(1, rows):
        total = total + got_row[index]
    summed[...] = total
    phase(
        1, "col", me_col, cols,
        lambda peer: summed.at[pl.ds(pl.multiple_of(peer * piece, piece), piece)], got_col,
    )
    total = got_col[0]
    for index in range(1, cols):
        total = total + got_col[index]
    reduced[...] = total
    phase(2, "col", me_col, cols, lambda peer: reduced, gathered)
    phase(3, "row", me_row, rows, lambda peer: gathered, out_ref)


def all_sum(parts):
    both = jnp.stack(parts, 0)
    rows, cols = lax.axis_size("row"), lax.axis_size("col")
    lanes = 128
    piece = -(-both.size // (rows * cols * lanes))
    piece = -(-piece // 8) * 8
    chunk = cols * piece * lanes
    padded_size = rows * chunk
    flat = jnp.pad(both.reshape(-1), (0, padded_size - both.size))
    count = max(rows, cols)
    out = pl.pallas_call(
        functools.partial(reduce_kernel, rows, cols),
        out_shape=jax.ShapeDtypeStruct((rows, cols, piece, lanes), jnp.float32),
        in_specs=[pl.BlockSpec(memory_space=pltpu.VMEM)],
        out_specs=pl.BlockSpec(memory_space=pltpu.VMEM),
        scratch_shapes=[
            pltpu.VMEM((rows, cols * piece, lanes), jnp.float32),
            pltpu.VMEM((cols * piece, lanes), jnp.float32),
            pltpu.VMEM((cols, piece, lanes), jnp.float32),
            pltpu.VMEM((piece, lanes), jnp.float32),
            pltpu.VMEM((cols, piece, lanes), jnp.float32),
            pltpu.SemaphoreType.DMA((4, count)),
            pltpu.SemaphoreType.DMA((4, count)),
            pltpu.SemaphoreType.DMA((4,)),
        ],
        compiler_params=pltpu.CompilerParams(collective_id=0, has_side_effects=True),
    )(flat.reshape(rows, cols * piece, lanes))
    return out.reshape(-1)[: both.size].reshape(both.shape)


def local(frames, state, input_weight, state_weight, cotangent):
    step_count = frames.shape[0]
    channels = state.shape[0]
    rows, cols = state.shape[1], state.shape[2]
    halo = HALO
    ext_rows, ext_cols = rows + 2 * halo, cols + 2 * halo
    length = ext_rows * ext_cols
    reach = ext_cols + 1
    offsets = [(k // 3 - 1) * ext_cols + (k % 3 - 1) for k in range(9)]
    tile = (halo * ext_cols, (halo + rows) * ext_cols)
    spans = [(tile[0] - depth * reach, tile[1] + depth * reach) for depth in range(2 * step_count)]
    forward_spans = spans[2 * step_count - 1 :: -1][:step_count]
    backward_spans = spans[step_count : 0 : -1]

    fields = jnp.concatenate([frames.reshape(-1, rows, cols), state, cotangent], 0)
    fields = padded_2(fields, (("row", 1), ("col", 2)), halo).reshape(-1, length)
    padded = jnp.pad(fields, ((0, 0), (reach, reach)))
    frame_pad = [padded[t * frames.shape[1] : (t + 1) * frames.shape[1]] for t in range(step_count)]
    base = step_count * frames.shape[1]
    state_pad = padded[base : base + channels]
    cot_flat = fields[base + channels :]

    r = lax.broadcasted_iota(jnp.int32, (ext_rows, ext_cols), 0)
    c = lax.broadcasted_iota(jnp.int32, (ext_rows, ext_cols), 1)
    global_r = lax.axis_index("row") * rows + r - halo
    global_c = lax.axis_index("col") * cols + c - halo
    inside = (
        (global_r >= 0)
        & (global_r < rows * lax.axis_size("row"))
        & (global_c >= 0)
        & (global_c < cols * lax.axis_size("col"))
    ).reshape(1, length)
    own = ((r >= halo) & (r < halo + rows) & (c >= halo) & (c < halo + cols)).reshape(1, length)

    records = []
    current, current_start = state_pad, -reach
    for step_index in range(step_count):
        span = forward_spans[step_index]
        from_input = conv_flat(input_weight, frame_pad[step_index], -reach, span, offsets)
        from_state = conv_flat(state_weight, current, current_start, span, offsets)
        previous = cut(current, current_start, span)
        new_state, saved = gates(from_input, from_state, previous, channels)
        records.append((current, current_start, span, saved))
        current = jnp.where(cut(inside, 0, span), new_state, jnp.zeros_like(new_state))
        current_start = span[0]
    final_state = cut(current, current_start, tile)

    grad_state, grad_start = cot_flat, 0
    input_sum = None
    state_sum = None
    for step_index in reversed(range(step_count)):
        field, field_start, forward_span, saved = records[step_index]
        span = backward_spans[step_count - 1 - step_index]
        saved = tuple(cut(value, forward_span[0], span) for value in saved)
        previous = cut(field, field_start, span)
        input_pre, state_pre, direct = gate_grads(
            cut(grad_state, grad_start, span).astype(jnp.float32), saved, previous
        )
        keep = cut(own, 0, tile)
        input_tile = cut(input_pre, span[0], tile)
        state_tile = cut(state_pre, span[0], tile)
        input_share = weight_flat(
            jnp.where(keep, input_tile, jnp.zeros_like(input_tile)), frame_pad[step_index], -reach, tile, offsets
        )
        state_share = weight_flat(
            jnp.where(keep, state_tile, jnp.zeros_like(state_tile)), field, field_start, tile, offsets
        )
        input_sum = input_share if input_sum is None else input_sum + input_share
        state_sum = state_share if state_sum is None else state_sum + state_share
        state_pre = jnp.where(cut(inside, 0, span), state_pre, jnp.zeros_like(state_pre))
        inner = (span[0] + reach, span[1] - reach)
        grad_state = cut(direct, span[0], inner) + spread_flat(state_weight, state_pre, span[0], inner, offsets)
        grad_start = inner[0]

    input_sum, state_sum = all_sum([input_sum, state_sum])
    loss_scale = (rows * lax.axis_size("row") * cols * lax.axis_size("col")) ** (-0.5)

    def crop(flat):
        return flat.reshape(flat.shape[0], rows, ext_cols)[:, :, halo : halo + cols]

    return (crop(final_state), crop(grad_state), input_sum * loss_scale, state_sum * loss_scale)


def solution(mesh):
    in_specs = (P(None, None, "row", "col"), P(None, "row", "col"), P(), P(), P(None, "row", "col"))
    out_specs = (P(None, "row", "col"), P(None, "row", "col"), P(), P())
    return jax.shard_map(local, mesh=mesh, in_specs=in_specs, out_specs=out_specs, check_vma=False)
```

```python
import functools

import jax
import jax.numpy as jnp
from jax import lax
from jax.experimental import pallas as pl
from jax.experimental.pallas import tpu as pltpu
from jax.sharding import PartitionSpec as P

HALO = 4


def padded_2(array, sides, width):
    for axis, dim in sides:
        devices, length = (lax.axis_size(axis), array.shape[dim])
        up = [(i, (i + 1) % devices) for i in range(devices - 1)]
        down = [(j, i) for i, j in up]
        last = lax.slice_in_dim(array, length - width, length, axis=dim)
        first = lax.slice_in_dim(array, 0, width, axis=dim)
        before = lax.ppermute(last, axis, up)
        after = lax.ppermute(first, axis, down)
        array = jnp.concatenate([before, array, after], axis=dim)
    return array


def shifted(flat, offsets, margin, length):
    return jnp.concatenate([flat[:, margin + off : margin + off + length] for off in offsets], 0)


def conv_flat(weights, flat, offsets, margin, length):
    taps, out_ch, in_ch = weights.shape
    stack = shifted(flat, offsets, margin, length)
    matrix = weights.transpose(1, 0, 2).reshape(out_ch, taps * in_ch)
    return jnp.dot(matrix, stack, preferred_element_type=jnp.float32)


def spread_flat(weights, flat, offsets, margin, length):
    taps, out_ch, in_ch = weights.shape
    stack = shifted(flat, [-off for off in offsets], margin, length)
    matrix = weights.transpose(2, 0, 1).reshape(in_ch, taps * out_ch)
    return jnp.dot(matrix, stack, preferred_element_type=jnp.float32)


def weight_flat(pre_grad, flat, offsets, margin, length):
    taps = len(offsets)
    stack = shifted(flat, offsets, margin, length)
    share = lax.dot_general(
        pre_grad, stack, (((1,), (1,)), ((), ())), preferred_element_type=jnp.float32
    )
    return share


def gates(from_input, from_state, previous, channels):
    update = jax.nn.sigmoid(from_input[:channels] + from_state[:channels])
    reset_gate = jax.nn.sigmoid(
        from_input[channels : 2 * channels] + from_state[channels : 2 * channels]
    )
    state_term = from_state[2 * channels :]
    candidate = jnp.tanh(from_input[2 * channels :] + reset_gate * state_term)
    new_state = ((1.0 - update) * candidate + update * previous.astype(jnp.float32)).astype(
        jnp.bfloat16
    )
    return new_state, (update, reset_gate, candidate, state_term)


def gate_grads(grad_state, saved, previous):
    update, reset_gate, candidate, state_term = saved
    grad_candidate = grad_state * (1.0 - update)
    grad_update = grad_state * (previous.astype(jnp.float32) - candidate)
    pre_update = grad_update * update * (1.0 - update)
    pre_candidate = grad_candidate * (1.0 - candidate * candidate)
    pre_reset = pre_candidate * state_term * reset_gate * (1.0 - reset_gate)
    pre_hidden = pre_candidate * reset_gate
    input_pre = jnp.concatenate([pre_update, pre_reset, pre_candidate], 0).astype(jnp.bfloat16)
    state_pre = jnp.concatenate([pre_update, pre_reset, pre_hidden], 0).astype(jnp.bfloat16)
    return (input_pre, state_pre, grad_state * update)


def reduce_kernel(rows, cols, x_ref, out_ref, got_row, summed, got_col, reduced, send_sem, recv_sem, own_sem):
    mesh_ids = pl.DeviceIdType.MESH
    me_row, me_col = lax.axis_index("row"), lax.axis_index("col")
    barrier = pltpu.get_barrier_semaphore()
    for axis, me, count in (("row", me_row, rows), ("col", me_col, cols)):
        for distance in range(1, count):
            peer = lax.rem(me + distance, count)
            pl.semaphore_signal(barrier, inc=1, device_id={axis: peer}, device_id_type=mesh_ids)
    pl.semaphore_wait(barrier, rows + cols - 2)
    chunk = summed.shape[0]

    def phase(index, axis, me, count, source, target):
        copies = []
        for distance in range(1, count):
            peer = lax.rem(me + distance, count)
            copy = pltpu.make_async_remote_copy(
                src_ref=source(peer),
                dst_ref=target.at[me],
                send_sem=send_sem.at[index, distance],
                recv_sem=recv_sem.at[index, distance],
                device_id={axis: peer},
                device_id_type=mesh_ids,
            )
            copy.start()
            copies.append(copy)
        own = pltpu.make_async_copy(source(me), target.at[me], own_sem.at[index])
        own.start()
        own.wait()
        for copy in copies:
            copy.wait()

    phase(0, "row", me_row, rows, lambda peer: x_ref.at[pl.ds(pl.multiple_of(peer * chunk, 8), chunk)], got_row)
    total = got_row[0]
    for index in range(1, rows):
        total = total + got_row[index]
    summed[...] = total
    phase(1, "col", me_col, cols, lambda peer: summed, got_col)
    total = got_col[0]
    for index in range(1, cols):
        total = total + got_col[index]
    reduced[...] = total
    phase(2, "row", me_row, rows, lambda peer: reduced, out_ref)


def all_sum(parts):
    both = jnp.concatenate(parts, 0)
    rows, cols = lax.axis_size("row"), lax.axis_size("col")
    chunk = both.shape[0] // rows
    width = both.shape[1]
    count = max(rows, cols)
    out = pl.pallas_call(
        functools.partial(reduce_kernel, rows, cols),
        out_shape=jax.ShapeDtypeStruct((rows, chunk, width), jnp.float32),
        in_specs=[pl.BlockSpec(memory_space=pltpu.VMEM)],
        out_specs=pl.BlockSpec(memory_space=pltpu.VMEM),
        scratch_shapes=[
            pltpu.VMEM((rows, chunk, width), jnp.float32),
            pltpu.VMEM((chunk, width), jnp.float32),
            pltpu.VMEM((cols, chunk, width), jnp.float32),
            pltpu.VMEM((chunk, width), jnp.float32),
            pltpu.SemaphoreType.DMA((3, count)),
            pltpu.SemaphoreType.DMA((3, count)),
            pltpu.SemaphoreType.DMA((3,)),
        ],
        compiler_params=pltpu.CompilerParams(collective_id=0, has_side_effects=True),
    )(both)
    return jnp.split(out.reshape(both.shape), len(parts), 0)


def local(frames, state, input_weight, state_weight, cotangent):
    step_count = frames.shape[0]
    channels = state.shape[0]
    rows, cols = state.shape[1], state.shape[2]
    halo = HALO
    ext_rows, ext_cols = rows + 2 * halo, cols + 2 * halo
    length = ext_rows * ext_cols
    margin = ext_cols + 1
    offsets = [(k // 3 - 1) * ext_cols + (k % 3 - 1) for k in range(9)]

    fields = jnp.concatenate([frames.reshape(-1, rows, cols), state, cotangent], 0)
    fields = padded_2(fields, (("row", 1), ("col", 2)), halo).reshape(-1, length)
    frame_flat = [fields[t * frames.shape[1] : (t + 1) * frames.shape[1]] for t in range(step_count)]
    base = step_count * frames.shape[1]
    state_flat = fields[base : base + channels]
    cot_flat = fields[base + channels :]

    r = lax.broadcasted_iota(jnp.int32, (ext_rows, ext_cols), 0)
    c = lax.broadcasted_iota(jnp.int32, (ext_rows, ext_cols), 1)
    global_r = lax.axis_index("row") * rows + r - halo
    global_c = lax.axis_index("col") * cols + c - halo
    inside = (
        (global_r >= 0)
        & (global_r < rows * lax.axis_size("row"))
        & (global_c >= 0)
        & (global_c < cols * lax.axis_size("col"))
    ).reshape(1, length)
    own = ((r >= halo) & (r < halo + rows) & (c >= halo) & (c < halo + cols)).reshape(1, length)

    def pad(flat):
        return jnp.pad(flat, ((0, 0), (margin, margin)))

    records = []
    current = state_flat
    for step_index in range(step_count):
        frame_pad, state_pad = pad(frame_flat[step_index]), pad(current)
        from_input = conv_flat(input_weight, frame_pad, offsets, margin, length)
        from_state = conv_flat(state_weight, state_pad, offsets, margin, length)
        new_state, saved = gates(from_input, from_state, current, channels)
        records.append((frame_pad, state_pad, current, saved))
        current = jnp.where(inside, new_state, jnp.zeros_like(new_state))

    grad_state = cot_flat.astype(jnp.float32)
    input_pres, input_fields, state_pres, state_fields = [], [], [], []
    for step_index in reversed(range(step_count)):
        frame_pad, state_pad, previous, saved = records[step_index]
        input_pre, state_pre, direct = gate_grads(grad_state, saved, previous)
        input_pres.append(jnp.where(own, input_pre, jnp.zeros_like(input_pre)))
        state_pres.append(jnp.where(own, state_pre, jnp.zeros_like(state_pre)))
        input_fields.append(frame_pad)
        state_fields.append(state_pad)
        state_pre = jnp.where(inside, state_pre, jnp.zeros_like(state_pre))
        grad_state = direct + spread_flat(state_weight, pad(state_pre), offsets, margin, length)

    input_sum = sum(
        weight_flat(p, f, offsets, margin, length) for p, f in zip(input_pres, input_fields)
    )
    state_sum = sum(
        weight_flat(p, f, offsets, margin, length) for p, f in zip(state_pres, state_fields)
    )
    input_sum, state_sum = all_sum([input_sum, state_sum])
    taps, out_ch, in_ch = input_weight.shape
    input_sum = input_sum.reshape(out_ch, taps, in_ch).transpose(1, 0, 2)
    taps, out_ch, in_ch = state_weight.shape
    state_sum = state_sum.reshape(out_ch, taps, in_ch).transpose(1, 0, 2)
    loss_scale = (rows * lax.axis_size("row") * cols * lax.axis_size("col")) ** (-0.5)

    def crop(flat):
        return flat.reshape(-1, ext_rows, ext_cols)[:, halo : halo + rows, halo : halo + cols]

    return (crop(current), crop(grad_state), input_sum * loss_scale, state_sum * loss_scale)


def solution(mesh):
    in_specs = (P(None, None, "row", "col"), P(None, "row", "col"), P(), P(), P(None, "row", "col"))
    out_specs = (P(None, "row", "col"), P(None, "row", "col"), P(), P())
    return jax.shard_map(local, mesh=mesh, in_specs=in_specs, out_specs=out_specs, check_vma=False)
```

```python
import functools

import jax
import jax.numpy as jnp
from jax import lax
from jax.experimental import pallas as pl
from jax.experimental.pallas import tpu as pltpu
from jax.sharding import PartitionSpec as P

HALO = 4


def padded_2(array, sides, width):
    for axis, dim in sides:
        devices, length = (lax.axis_size(axis), array.shape[dim])
        up = [(i, (i + 1) % devices) for i in range(devices - 1)]
        down = [(j, i) for i, j in up]
        last = lax.slice_in_dim(array, length - width, length, axis=dim)
        first = lax.slice_in_dim(array, 0, width, axis=dim)
        before = lax.ppermute(last, axis, up)
        after = lax.ppermute(first, axis, down)
        array = jnp.concatenate([before, array, after], axis=dim)
    return array


def shifted(flat, offsets, margin, length):
    return jnp.concatenate([flat[:, margin + off : margin + off + length] for off in offsets], 0)


def conv_flat(weights, flat, offsets, margin, length):
    taps, out_ch, in_ch = weights.shape
    stack = shifted(flat, offsets, margin, length)
    matrix = weights.transpose(1, 0, 2).reshape(out_ch, taps * in_ch)
    return jnp.dot(matrix, stack, preferred_element_type=jnp.float32)


def spread_flat(weights, flat, offsets, margin, length):
    taps, out_ch, in_ch = weights.shape
    stack = shifted(flat, [-off for off in offsets], margin, length)
    matrix = weights.transpose(2, 0, 1).reshape(in_ch, taps * out_ch)
    return jnp.dot(matrix, stack, preferred_element_type=jnp.float32)


def weight_flat(pre_grad, flat, offsets, margin, length):
    taps = len(offsets)
    stack = shifted(flat, offsets, margin, length)
    share = lax.dot_general(
        pre_grad, stack, (((1,), (1,)), ((), ())), preferred_element_type=jnp.float32
    )
    return share


def gates(from_input, from_state, previous, channels):
    update = jax.nn.sigmoid(from_input[:channels] + from_state[:channels])
    reset_gate = jax.nn.sigmoid(
        from_input[channels : 2 * channels] + from_state[channels : 2 * channels]
    )
    state_term = from_state[2 * channels :]
    candidate = jnp.tanh(from_input[2 * channels :] + reset_gate * state_term)
    new_state = ((1.0 - update) * candidate + update * previous.astype(jnp.float32)).astype(
        jnp.bfloat16
    )
    return new_state, (update, reset_gate, candidate, state_term)


def gate_grads(grad_state, saved, previous):
    update, reset_gate, candidate, state_term = saved
    grad_candidate = grad_state * (1.0 - update)
    grad_update = grad_state * (previous.astype(jnp.float32) - candidate)
    pre_update = grad_update * update * (1.0 - update)
    pre_candidate = grad_candidate * (1.0 - candidate * candidate)
    pre_reset = pre_candidate * state_term * reset_gate * (1.0 - reset_gate)
    pre_hidden = pre_candidate * reset_gate
    input_pre = jnp.concatenate([pre_update, pre_reset, pre_candidate], 0).astype(jnp.bfloat16)
    state_pre = jnp.concatenate([pre_update, pre_reset, pre_hidden], 0).astype(jnp.bfloat16)
    return (input_pre, state_pre, grad_state * update)


def reduce_kernel(rows, cols, x_ref, out_ref, got_row, summed, got_col, reduced, gathered, send_sem, recv_sem, own_sem):
    mesh_ids = pl.DeviceIdType.MESH
    me_row, me_col = lax.axis_index("row"), lax.axis_index("col")
    barrier = pltpu.get_barrier_semaphore()
    for axis, me, count in (("row", me_row, rows), ("col", me_col, cols)):
        for distance in range(1, count):
            peer = lax.rem(me + distance, count)
            pl.semaphore_signal(barrier, inc=1, device_id={axis: peer}, device_id_type=mesh_ids)
    pl.semaphore_wait(barrier, rows + cols - 2)
    piece = summed.shape[0] // cols

    def phase(index, axis, me, count, source, target):
        copies = []
        for distance in range(1, count):
            peer = lax.rem(me + distance, count)
            copy = pltpu.make_async_remote_copy(
                src_ref=source(peer),
                dst_ref=target.at[me],
                send_sem=send_sem.at[index, distance],
                recv_sem=recv_sem.at[index, distance],
                device_id={axis: peer},
                device_id_type=mesh_ids,
            )
            copy.start()
            copies.append(copy)
        own = pltpu.make_async_copy(source(me), target.at[me], own_sem.at[index])
        own.start()
        own.wait()
        for copy in copies:
            copy.wait()

    phase(0, "row", me_row, rows, lambda peer: x_ref.at[peer], got_row)
    total = got_row[0]
    for index in range(1, rows):
        total = total + got_row[index]
    summed[...] = total
    phase(
        1, "col", me_col, cols,
        lambda peer: summed.at[pl.ds(pl.multiple_of(peer * piece, piece), piece)], got_col,
    )
    total = got_col[0]
    for index in range(1, cols):
        total = total + got_col[index]
    reduced[...] = total
    phase(2, "col", me_col, cols, lambda peer: reduced, gathered)
    phase(3, "row", me_row, rows, lambda peer: gathered, out_ref)


def all_sum(parts):
    both = jnp.concatenate(parts, 0)
    rows, cols = lax.axis_size("row"), lax.axis_size("col")
    lanes = 128
    piece = -(-both.size // (rows * cols * lanes))
    piece = -(-piece // 8) * 8
    chunk = cols * piece * lanes
    padded_size = rows * chunk
    flat = jnp.pad(both.reshape(-1), (0, padded_size - both.size))
    count = max(rows, cols)
    out = pl.pallas_call(
        functools.partial(reduce_kernel, rows, cols),
        out_shape=jax.ShapeDtypeStruct((rows, cols, piece, lanes), jnp.float32),
        in_specs=[pl.BlockSpec(memory_space=pltpu.VMEM)],
        out_specs=pl.BlockSpec(memory_space=pltpu.VMEM),
        scratch_shapes=[
            pltpu.VMEM((rows, cols * piece, lanes), jnp.float32),
            pltpu.VMEM((cols * piece, lanes), jnp.float32),
            pltpu.VMEM((cols, piece, lanes), jnp.float32),
            pltpu.VMEM((piece, lanes), jnp.float32),
            pltpu.VMEM((cols, piece, lanes), jnp.float32),
            pltpu.SemaphoreType.DMA((4, count)),
            pltpu.SemaphoreType.DMA((4, count)),
            pltpu.SemaphoreType.DMA((4,)),
        ],
        compiler_params=pltpu.CompilerParams(collective_id=0, has_side_effects=True),
    )(flat.reshape(rows, cols * piece, lanes))
    return jnp.split(out.reshape(-1)[: both.size].reshape(both.shape), len(parts), 0)


def local(frames, state, input_weight, state_weight, cotangent):
    step_count = frames.shape[0]
    channels = state.shape[0]
    rows, cols = state.shape[1], state.shape[2]
    halo = HALO
    ext_rows, ext_cols = rows + 2 * halo, cols + 2 * halo
    length = ext_rows * ext_cols
    margin = ext_cols + 1
    offsets = [(k // 3 - 1) * ext_cols + (k % 3 - 1) for k in range(9)]

    fields = jnp.concatenate([frames.reshape(-1, rows, cols), state, cotangent], 0)
    fields = padded_2(fields, (("row", 1), ("col", 2)), halo).reshape(-1, length)
    frame_flat = [fields[t * frames.shape[1] : (t + 1) * frames.shape[1]] for t in range(step_count)]
    base = step_count * frames.shape[1]
    state_flat = fields[base : base + channels]
    cot_flat = fields[base + channels :]

    r = lax.broadcasted_iota(jnp.int32, (ext_rows, ext_cols), 0)
    c = lax.broadcasted_iota(jnp.int32, (ext_rows, ext_cols), 1)
    global_r = lax.axis_index("row") * rows + r - halo
    global_c = lax.axis_index("col") * cols + c - halo
    inside = (
        (global_r >= 0)
        & (global_r < rows * lax.axis_size("row"))
        & (global_c >= 0)
        & (global_c < cols * lax.axis_size("col"))
    ).reshape(1, length)
    own = ((r >= halo) & (r < halo + rows) & (c >= halo) & (c < halo + cols)).reshape(1, length)

    def pad(flat):
        return jnp.pad(flat, ((0, 0), (margin, margin)))

    records = []
    current = state_flat
    for step_index in range(step_count):
        frame_pad, state_pad = pad(frame_flat[step_index]), pad(current)
        from_input = conv_flat(input_weight, frame_pad, offsets, margin, length)
        from_state = conv_flat(state_weight, state_pad, offsets, margin, length)
        new_state, saved = gates(from_input, from_state, current, channels)
        records.append((frame_pad, state_pad, current, saved))
        current = jnp.where(inside, new_state, jnp.zeros_like(new_state))

    grad_state = cot_flat.astype(jnp.float32)
    input_pres, input_fields, state_pres, state_fields = [], [], [], []
    for step_index in reversed(range(step_count)):
        frame_pad, state_pad, previous, saved = records[step_index]
        input_pre, state_pre, direct = gate_grads(grad_state, saved, previous)
        input_pres.append(jnp.where(own, input_pre, jnp.zeros_like(input_pre)))
        state_pres.append(jnp.where(own, state_pre, jnp.zeros_like(state_pre)))
        input_fields.append(frame_pad)
        state_fields.append(state_pad)
        state_pre = jnp.where(inside, state_pre, jnp.zeros_like(state_pre))
        grad_state = direct + spread_flat(state_weight, pad(state_pre), offsets, margin, length)

    input_sum = sum(
        weight_flat(p, f, offsets, margin, length) for p, f in zip(input_pres, input_fields)
    )
    state_sum = sum(
        weight_flat(p, f, offsets, margin, length) for p, f in zip(state_pres, state_fields)
    )
    input_sum, state_sum = all_sum([input_sum, state_sum])
    taps, out_ch, in_ch = input_weight.shape
    input_sum = input_sum.reshape(out_ch, taps, in_ch).transpose(1, 0, 2)
    taps, out_ch, in_ch = state_weight.shape
    state_sum = state_sum.reshape(out_ch, taps, in_ch).transpose(1, 0, 2)
    loss_scale = (rows * lax.axis_size("row") * cols * lax.axis_size("col")) ** (-0.5)

    def crop(flat):
        return flat.reshape(-1, ext_rows, ext_cols)[:, halo : halo + rows, halo : halo + cols]

    return (crop(current), crop(grad_state), input_sum * loss_scale, state_sum * loss_scale)


def solution(mesh):
    in_specs = (P(None, None, "row", "col"), P(None, "row", "col"), P(), P(), P(None, "row", "col"))
    out_specs = (P(None, "row", "col"), P(None, "row", "col"), P(), P())
    return jax.shard_map(local, mesh=mesh, in_specs=in_specs, out_specs=out_specs, check_vma=False)
```

```python
import functools

import jax
import jax.numpy as jnp
from jax import lax
from jax.experimental import pallas as pl
from jax.experimental.pallas import tpu as pltpu
from jax.sharding import PartitionSpec as P

HALO = 4


def padded_2(array, sides, width):
    for axis, dim in sides:
        devices, length = (lax.axis_size(axis), array.shape[dim])
        up = [(i, (i + 1) % devices) for i in range(devices - 1)]
        down = [(j, i) for i, j in up]
        last = lax.slice_in_dim(array, length - width, length, axis=dim)
        first = lax.slice_in_dim(array, 0, width, axis=dim)
        before = lax.ppermute(last, axis, up)
        after = lax.ppermute(first, axis, down)
        array = jnp.concatenate([before, array, after], axis=dim)
    return array


def shifted(flat, offsets, margin, length):
    return jnp.concatenate([flat[:, margin + off : margin + off + length] for off in offsets], 0)


def conv_flat(weights, flat, offsets, margin, length):
    taps, out_ch, in_ch = weights.shape
    stack = shifted(flat, offsets, margin, length)
    matrix = weights.transpose(1, 0, 2).reshape(out_ch, taps * in_ch)
    return jnp.dot(matrix, stack, preferred_element_type=jnp.float32)


def spread_flat(weights, flat, offsets, margin, length):
    taps, out_ch, in_ch = weights.shape
    stack = shifted(flat, [-off for off in offsets], margin, length)
    matrix = weights.transpose(2, 0, 1).reshape(in_ch, taps * out_ch)
    return jnp.dot(matrix, stack, preferred_element_type=jnp.float32)


def weight_flat(pre_grad, flat, offsets, margin, length):
    taps = len(offsets)
    stack = shifted(flat, offsets, margin, length)
    share = lax.dot_general(
        pre_grad, stack, (((1,), (1,)), ((), ())), preferred_element_type=jnp.float32
    )
    return share


def gates(from_input, from_state, previous, channels):
    update = jax.nn.sigmoid(from_input[:channels] + from_state[:channels])
    reset_gate = jax.nn.sigmoid(
        from_input[channels : 2 * channels] + from_state[channels : 2 * channels]
    )
    state_term = from_state[2 * channels :]
    candidate = jnp.tanh(from_input[2 * channels :] + reset_gate * state_term)
    new_state = ((1.0 - update) * candidate + update * previous.astype(jnp.float32)).astype(
        jnp.bfloat16
    )
    return new_state, (update, reset_gate, candidate, state_term)


def gate_grads(grad_state, saved, previous):
    update, reset_gate, candidate, state_term = saved
    grad_candidate = grad_state * (1.0 - update)
    grad_update = grad_state * (previous.astype(jnp.float32) - candidate)
    pre_update = grad_update * update * (1.0 - update)
    pre_candidate = grad_candidate * (1.0 - candidate * candidate)
    pre_reset = pre_candidate * state_term * reset_gate * (1.0 - reset_gate)
    pre_hidden = pre_candidate * reset_gate
    input_pre = jnp.concatenate([pre_update, pre_reset, pre_candidate], 0).astype(jnp.bfloat16)
    state_pre = jnp.concatenate([pre_update, pre_reset, pre_hidden], 0).astype(jnp.bfloat16)
    return (input_pre, state_pre, grad_state * update)


def reduce_kernel(rows, cols, x_ref, out_ref, got_row, summed, got_col, reduced, gathered, send_sem, recv_sem, own_sem):
    mesh_ids = pl.DeviceIdType.MESH
    me_row, me_col = lax.axis_index("row"), lax.axis_index("col")
    barrier = pltpu.get_barrier_semaphore()
    for axis, me, count in (("row", me_row, rows), ("col", me_col, cols)):

        def greet(distance, carry, axis=axis, me=me, count=count):
            peer = lax.rem(me + distance, count)
            pl.semaphore_signal(barrier, inc=1, device_id={axis: peer}, device_id_type=mesh_ids)
            return carry

        lax.fori_loop(1, count, greet, 0)
    pl.semaphore_wait(barrier, rows + cols - 2)
    piece = summed.shape[0] // cols

    def phase(index, axis, me, count, source, target):
        def copy_to(distance):
            peer = lax.rem(me + distance, count)
            return pltpu.make_async_remote_copy(
                src_ref=source(peer),
                dst_ref=target.at[me],
                send_sem=send_sem.at[index, distance],
                recv_sem=recv_sem.at[index, distance],
                device_id={axis: peer},
                device_id_type=mesh_ids,
            )

        def start(distance, carry):
            copy_to(distance).start()
            return carry

        def finish(distance, carry):
            copy_to(distance).wait()
            return carry

        lax.fori_loop(1, count, start, 0)
        own = pltpu.make_async_copy(source(me), target.at[me], own_sem.at[index])
        own.start()
        own.wait()
        lax.fori_loop(1, count, finish, 0)

    def total_of(buffer, count):
        return lax.fori_loop(1, count, lambda index, acc: acc + buffer[index], buffer[0])

    phase(0, "row", me_row, rows, lambda peer: x_ref.at[peer], got_row)
    summed[...] = total_of(got_row, rows)
    phase(
        1, "col", me_col, cols,
        lambda peer: summed.at[pl.ds(pl.multiple_of(peer * piece, piece), piece)], got_col,
    )
    reduced[...] = total_of(got_col, cols)
    phase(2, "col", me_col, cols, lambda peer: reduced, gathered)
    phase(3, "row", me_row, rows, lambda peer: gathered, out_ref)


def all_sum(parts):
    both = jnp.concatenate(parts, 0)
    rows, cols = lax.axis_size("row"), lax.axis_size("col")
    lanes = 128
    piece = -(-both.size // (rows * cols * lanes))
    piece = -(-piece // 8) * 8
    chunk = cols * piece * lanes
    padded_size = rows * chunk
    flat = jnp.pad(both.reshape(-1), (0, padded_size - both.size))
    count = max(rows, cols)
    out = pl.pallas_call(
        functools.partial(reduce_kernel, rows, cols),
        out_shape=jax.ShapeDtypeStruct((rows, cols, piece, lanes), jnp.float32),
        in_specs=[pl.BlockSpec(memory_space=pltpu.VMEM)],
        out_specs=pl.BlockSpec(memory_space=pltpu.VMEM),
        scratch_shapes=[
            pltpu.VMEM((rows, cols * piece, lanes), jnp.float32),
            pltpu.VMEM((cols * piece, lanes), jnp.float32),
            pltpu.VMEM((cols, piece, lanes), jnp.float32),
            pltpu.VMEM((piece, lanes), jnp.float32),
            pltpu.VMEM((cols, piece, lanes), jnp.float32),
            pltpu.SemaphoreType.DMA((4, count)),
            pltpu.SemaphoreType.DMA((4, count)),
            pltpu.SemaphoreType.DMA((4,)),
        ],
        compiler_params=pltpu.CompilerParams(collective_id=0, has_side_effects=True),
    )(flat.reshape(rows, cols * piece, lanes))
    return jnp.split(out.reshape(-1)[: both.size].reshape(both.shape), len(parts), 0)


def local(frames, state, input_weight, state_weight, cotangent):
    step_count = frames.shape[0]
    channels = state.shape[0]
    rows, cols = state.shape[1], state.shape[2]
    halo = HALO
    ext_rows, ext_cols = rows + 2 * halo, cols + 2 * halo
    length = ext_rows * ext_cols
    margin = ext_cols + 1
    offsets = [(k // 3 - 1) * ext_cols + (k % 3 - 1) for k in range(9)]

    fields = jnp.concatenate([frames.reshape(-1, rows, cols), state, cotangent], 0)
    fields = padded_2(fields, (("row", 1), ("col", 2)), halo).reshape(-1, length)
    frame_flat = [fields[t * frames.shape[1] : (t + 1) * frames.shape[1]] for t in range(step_count)]
    base = step_count * frames.shape[1]
    state_flat = fields[base : base + channels]
    cot_flat = fields[base + channels :]

    r = lax.broadcasted_iota(jnp.int32, (ext_rows, ext_cols), 0)
    c = lax.broadcasted_iota(jnp.int32, (ext_rows, ext_cols), 1)
    global_r = lax.axis_index("row") * rows + r - halo
    global_c = lax.axis_index("col") * cols + c - halo
    inside = (
        (global_r >= 0)
        & (global_r < rows * lax.axis_size("row"))
        & (global_c >= 0)
        & (global_c < cols * lax.axis_size("col"))
    ).reshape(1, length)
    own = ((r >= halo) & (r < halo + rows) & (c >= halo) & (c < halo + cols)).reshape(1, length)

    def pad(flat):
        return jnp.pad(flat, ((0, 0), (margin, margin)))

    records = []
    current = state_flat
    for step_index in range(step_count):
        frame_pad, state_pad = pad(frame_flat[step_index]), pad(current)
        from_input = conv_flat(input_weight, frame_pad, offsets, margin, length)
        from_state = conv_flat(state_weight, state_pad, offsets, margin, length)
        new_state, saved = gates(from_input, from_state, current, channels)
        records.append((frame_pad, state_pad, current, saved))
        current = jnp.where(inside, new_state, jnp.zeros_like(new_state))

    grad_state = cot_flat.astype(jnp.float32)
    input_pres, input_fields, state_pres, state_fields = [], [], [], []
    for step_index in reversed(range(step_count)):
        frame_pad, state_pad, previous, saved = records[step_index]
        input_pre, state_pre, direct = gate_grads(grad_state, saved, previous)
        input_pres.append(jnp.where(own, input_pre, jnp.zeros_like(input_pre)))
        state_pres.append(jnp.where(own, state_pre, jnp.zeros_like(state_pre)))
        input_fields.append(frame_pad)
        state_fields.append(state_pad)
        state_pre = jnp.where(inside, state_pre, jnp.zeros_like(state_pre))
        grad_state = direct + spread_flat(state_weight, pad(state_pre), offsets, margin, length)

    input_sum = sum(
        weight_flat(p, f, offsets, margin, length) for p, f in zip(input_pres, input_fields)
    )
    state_sum = sum(
        weight_flat(p, f, offsets, margin, length) for p, f in zip(state_pres, state_fields)
    )
    input_sum, state_sum = all_sum([input_sum, state_sum])
    taps, out_ch, in_ch = input_weight.shape
    input_sum = input_sum.reshape(out_ch, taps, in_ch).transpose(1, 0, 2)
    taps, out_ch, in_ch = state_weight.shape
    state_sum = state_sum.reshape(out_ch, taps, in_ch).transpose(1, 0, 2)
    loss_scale = (rows * lax.axis_size("row") * cols * lax.axis_size("col")) ** (-0.5)

    def crop(flat):
        return flat.reshape(-1, ext_rows, ext_cols)[:, halo : halo + rows, halo : halo + cols]

    return (crop(current), crop(grad_state), input_sum * loss_scale, state_sum * loss_scale)


def solution(mesh):
    in_specs = (P(None, None, "row", "col"), P(None, "row", "col"), P(), P(), P(None, "row", "col"))
    out_specs = (P(None, "row", "col"), P(None, "row", "col"), P(), P())
    return jax.shard_map(local, mesh=mesh, in_specs=in_specs, out_specs=out_specs, check_vma=False)
```

```python
import functools

import jax
import jax.numpy as jnp
from jax import lax
from jax.experimental import pallas as pl
from jax.experimental.pallas import tpu as pltpu
from jax.sharding import PartitionSpec as P

HALO = 4


def padded_2(array, sides, width):
    for axis, dim in sides:
        devices, length = (lax.axis_size(axis), array.shape[dim])
        up = [(i, (i + 1) % devices) for i in range(devices - 1)]
        down = [(j, i) for i, j in up]
        last = lax.slice_in_dim(array, length - width, length, axis=dim)
        first = lax.slice_in_dim(array, 0, width, axis=dim)
        before = lax.ppermute(last, axis, up)
        after = lax.ppermute(first, axis, down)
        array = jnp.concatenate([before, array, after], axis=dim)
    return array


def aligned_halo(array, width):
    array = padded_2(array, (("row", 1),), width)
    devices = lax.axis_size("col")
    up = [(i, i + 1) for i in range(devices - 1)]
    down = [(j, i) for i, j in up]
    left = lax.ppermute(array[:, :, -width:], "col", up)
    right = lax.ppermute(array[:, :, :width], "col", down)
    body = jnp.pad(jnp.concatenate([array, right], 2), ((0, 0), (1, 0), (0, 0)))
    left = jnp.pad(left, ((0, 0), (0, 1), (0, 0)))
    return jnp.concatenate([body, left], 2).reshape(array.shape[0], -1)


def shifted(flat, offsets, margin, length):
    return jnp.concatenate([flat[:, margin + off : margin + off + length] for off in offsets], 0)


def conv_flat(weights, flat, offsets, margin, length):
    taps, out_ch, in_ch = weights.shape
    stack = shifted(flat, offsets, margin, length)
    matrix = weights.transpose(1, 0, 2).reshape(out_ch, taps * in_ch)
    return jnp.dot(matrix, stack, preferred_element_type=jnp.float32)


def spread_flat(weights, flat, offsets, margin, length):
    taps, out_ch, in_ch = weights.shape
    stack = shifted(flat, [-off for off in offsets], margin, length)
    matrix = weights.transpose(2, 0, 1).reshape(in_ch, taps * out_ch)
    return jnp.dot(matrix, stack, preferred_element_type=jnp.float32)


def weight_flat(pre_grad, flat, offsets, margin, length):
    taps = len(offsets)
    stack = shifted(flat, offsets, margin, length)
    share = lax.dot_general(
        pre_grad, stack, (((1,), (1,)), ((), ())), preferred_element_type=jnp.float32
    )
    return share


def gates(from_input, from_state, previous, channels):
    update = jax.nn.sigmoid(from_input[:channels] + from_state[:channels])
    reset_gate = jax.nn.sigmoid(
        from_input[channels : 2 * channels] + from_state[channels : 2 * channels]
    )
    state_term = from_state[2 * channels :]
    candidate = jnp.tanh(from_input[2 * channels :] + reset_gate * state_term)
    new_state = ((1.0 - update) * candidate + update * previous.astype(jnp.float32)).astype(
        jnp.bfloat16
    )
    return new_state, (update, reset_gate, candidate, state_term)


def gate_grads(grad_state, saved, previous):
    update, reset_gate, candidate, state_term = saved
    grad_candidate = grad_state * (1.0 - update)
    grad_update = grad_state * (previous.astype(jnp.float32) - candidate)
    pre_update = grad_update * update * (1.0 - update)
    pre_candidate = grad_candidate * (1.0 - candidate * candidate)
    pre_reset = pre_candidate * state_term * reset_gate * (1.0 - reset_gate)
    pre_hidden = pre_candidate * reset_gate
    input_pre = jnp.concatenate([pre_update, pre_reset, pre_candidate], 0).astype(jnp.bfloat16)
    state_pre = jnp.concatenate([pre_update, pre_reset, pre_hidden], 0).astype(jnp.bfloat16)
    return (input_pre, state_pre, grad_state * update)


def reduce_kernel(rows, cols, x_ref, out_ref, got_row, summed, got_col, reduced, gathered, send_sem, recv_sem, own_sem):
    mesh_ids = pl.DeviceIdType.MESH
    me_row, me_col = lax.axis_index("row"), lax.axis_index("col")
    barrier = pltpu.get_barrier_semaphore()
    for axis, me, count in (("row", me_row, rows), ("col", me_col, cols)):

        def greet(distance, carry, axis=axis, me=me, count=count):
            peer = lax.rem(me + distance, count)
            pl.semaphore_signal(barrier, inc=1, device_id={axis: peer}, device_id_type=mesh_ids)
            return carry

        lax.fori_loop(1, count, greet, 0)
    pl.semaphore_wait(barrier, rows + cols - 2)
    piece = summed.shape[0] // cols

    def phase(index, axis, me, count, source, target):
        def copy_to(distance):
            peer = lax.rem(me + distance, count)
            return pltpu.make_async_remote_copy(
                src_ref=source(peer),
                dst_ref=target.at[me],
                send_sem=send_sem.at[index, distance],
                recv_sem=recv_sem.at[index, distance],
                device_id={axis: peer},
                device_id_type=mesh_ids,
            )

        def start(distance, carry):
            copy_to(distance).start()
            return carry

        def finish(distance, carry):
            copy_to(distance).wait()
            return carry

        lax.fori_loop(1, count, start, 0)
        own = pltpu.make_async_copy(source(me), target.at[me], own_sem.at[index])
        own.start()
        own.wait()
        lax.fori_loop(1, count, finish, 0)

    def total_of(buffer, count):
        return lax.fori_loop(1, count, lambda index, acc: acc + buffer[index], buffer[0])

    phase(0, "row", me_row, rows, lambda peer: x_ref.at[peer], got_row)
    summed[...] = total_of(got_row, rows)
    phase(
        1, "col", me_col, cols,
        lambda peer: summed.at[pl.ds(pl.multiple_of(peer * piece, piece), piece)], got_col,
    )
    reduced[...] = total_of(got_col, cols)
    phase(2, "col", me_col, cols, lambda peer: reduced, gathered)
    phase(3, "row", me_row, rows, lambda peer: gathered, out_ref)


def all_sum(parts):
    both = jnp.concatenate(parts, 0)
    rows, cols = lax.axis_size("row"), lax.axis_size("col")
    lanes = 128
    piece = -(-both.size // (rows * cols * lanes))
    piece = -(-piece // 8) * 8
    chunk = cols * piece * lanes
    padded_size = rows * chunk
    flat = jnp.pad(both.reshape(-1), (0, padded_size - both.size))
    count = max(rows, cols)
    out = pl.pallas_call(
        functools.partial(reduce_kernel, rows, cols),
        out_shape=jax.ShapeDtypeStruct((rows, cols, piece, lanes), jnp.float32),
        in_specs=[pl.BlockSpec(memory_space=pltpu.VMEM)],
        out_specs=pl.BlockSpec(memory_space=pltpu.VMEM),
        scratch_shapes=[
            pltpu.VMEM((rows, cols * piece, lanes), jnp.float32),
            pltpu.VMEM((cols * piece, lanes), jnp.float32),
            pltpu.VMEM((cols, piece, lanes), jnp.float32),
            pltpu.VMEM((piece, lanes), jnp.float32),
            pltpu.VMEM((cols, piece, lanes), jnp.float32),
            pltpu.SemaphoreType.DMA((4, count)),
            pltpu.SemaphoreType.DMA((4, count)),
            pltpu.SemaphoreType.DMA((4,)),
        ],
        compiler_params=pltpu.CompilerParams(collective_id=0, has_side_effects=True),
    )(flat.reshape(rows, cols * piece, lanes))
    return jnp.split(out.reshape(-1)[: both.size].reshape(both.shape), len(parts), 0)


def local(frames, state, input_weight, state_weight, cotangent):
    step_count = frames.shape[0]
    channels = state.shape[0]
    rows, cols = state.shape[1], state.shape[2]
    halo = HALO
    ext_rows, ext_cols = rows + 2 * halo, cols + 2 * halo
    length = ext_rows * ext_cols
    margin = ext_cols + 1
    offsets = [(k // 3 - 1) * ext_cols + (k % 3 - 1) for k in range(9)]

    fields = jnp.concatenate([frames.reshape(-1, rows, cols), state, cotangent], 0)
    lead = ext_cols - halo
    fields = aligned_halo(fields, halo)[:, lead : lead + length]
    frame_flat = [fields[t * frames.shape[1] : (t + 1) * frames.shape[1]] for t in range(step_count)]
    base = step_count * frames.shape[1]
    state_flat = fields[base : base + channels]
    cot_flat = fields[base + channels :]

    r = lax.broadcasted_iota(jnp.int32, (ext_rows, ext_cols), 0)
    c = lax.broadcasted_iota(jnp.int32, (ext_rows, ext_cols), 1)
    global_r = lax.axis_index("row") * rows + r - halo
    global_c = lax.axis_index("col") * cols + c - halo
    inside = (
        (global_r >= 0)
        & (global_r < rows * lax.axis_size("row"))
        & (global_c >= 0)
        & (global_c < cols * lax.axis_size("col"))
    ).reshape(1, length)
    own = ((r >= halo) & (r < halo + rows) & (c >= halo) & (c < halo + cols)).reshape(1, length)

    def pad(flat):
        return jnp.pad(flat, ((0, 0), (margin, margin)))

    records = []
    current = state_flat
    for step_index in range(step_count):
        frame_pad, state_pad = pad(frame_flat[step_index]), pad(current)
        from_input = conv_flat(input_weight, frame_pad, offsets, margin, length)
        from_state = conv_flat(state_weight, state_pad, offsets, margin, length)
        new_state, saved = gates(from_input, from_state, current, channels)
        records.append((frame_pad, state_pad, current, saved))
        current = jnp.where(inside, new_state, jnp.zeros_like(new_state))

    grad_state = cot_flat.astype(jnp.float32)
    input_pres, input_fields, state_pres, state_fields = [], [], [], []
    for step_index in reversed(range(step_count)):
        frame_pad, state_pad, previous, saved = records[step_index]
        input_pre, state_pre, direct = gate_grads(grad_state, saved, previous)
        input_pres.append(jnp.where(own, input_pre, jnp.zeros_like(input_pre)))
        state_pres.append(jnp.where(own, state_pre, jnp.zeros_like(state_pre)))
        input_fields.append(frame_pad)
        state_fields.append(state_pad)
        state_pre = jnp.where(inside, state_pre, jnp.zeros_like(state_pre))
        grad_state = direct + spread_flat(state_weight, pad(state_pre), offsets, margin, length)

    input_sum = sum(
        weight_flat(p, f, offsets, margin, length) for p, f in zip(input_pres, input_fields)
    )
    state_sum = sum(
        weight_flat(p, f, offsets, margin, length) for p, f in zip(state_pres, state_fields)
    )
    input_sum, state_sum = all_sum([input_sum, state_sum])
    taps, out_ch, in_ch = input_weight.shape
    input_sum = input_sum.reshape(out_ch, taps, in_ch).transpose(1, 0, 2)
    taps, out_ch, in_ch = state_weight.shape
    state_sum = state_sum.reshape(out_ch, taps, in_ch).transpose(1, 0, 2)
    loss_scale = (rows * lax.axis_size("row") * cols * lax.axis_size("col")) ** (-0.5)

    def crop(flat):
        return flat.reshape(-1, ext_rows, ext_cols)[:, halo : halo + rows, halo : halo + cols]

    return (crop(current), crop(grad_state), input_sum * loss_scale, state_sum * loss_scale)


def solution(mesh):
    in_specs = (P(None, None, "row", "col"), P(None, "row", "col"), P(), P(), P(None, "row", "col"))
    out_specs = (P(None, "row", "col"), P(None, "row", "col"), P(), P())
    return jax.shard_map(local, mesh=mesh, in_specs=in_specs, out_specs=out_specs, check_vma=False)
```

```python
import functools

import jax
import jax.numpy as jnp
from jax import lax
from jax.experimental import pallas as pl
from jax.experimental.pallas import tpu as pltpu
from jax.sharding import PartitionSpec as P

HALO = 4


def padded_2(array, sides, width):
    for axis, dim in sides:
        devices, length = (lax.axis_size(axis), array.shape[dim])
        up = [(i, (i + 1) % devices) for i in range(devices - 1)]
        down = [(j, i) for i, j in up]
        last = lax.slice_in_dim(array, length - width, length, axis=dim)
        first = lax.slice_in_dim(array, 0, width, axis=dim)
        before = lax.ppermute(last, axis, up)
        after = lax.ppermute(first, axis, down)
        array = jnp.concatenate([before, array, after], axis=dim)
    return array


def shifted(flat, offsets, margin, length):
    return jnp.concatenate([flat[:, margin + off : margin + off + length] for off in offsets], 0)


def conv_flat(weights, flat, offsets, margin, length):
    taps, out_ch, in_ch = weights.shape
    stack = shifted(flat, offsets, margin, length)
    matrix = weights.transpose(1, 0, 2).reshape(out_ch, taps * in_ch)
    return jnp.dot(matrix, stack, preferred_element_type=jnp.float32)


def spread_flat(weights, flat, offsets, margin, length):
    taps, out_ch, in_ch = weights.shape
    stack = shifted(flat, [-off for off in offsets], margin, length)
    matrix = weights.transpose(2, 0, 1).reshape(in_ch, taps * out_ch)
    return jnp.dot(matrix, stack, preferred_element_type=jnp.float32)


def weight_flat(pre_grad, flat, offsets, margin, length):
    taps = len(offsets)
    stack = shifted(flat, offsets, margin, length)
    share = lax.dot_general(
        pre_grad, stack, (((1,), (1,)), ((), ())), preferred_element_type=jnp.float32
    )
    return share


def gates(from_input, from_state, previous, channels):
    update = jax.nn.sigmoid(from_input[:channels] + from_state[:channels])
    reset_gate = jax.nn.sigmoid(
        from_input[channels : 2 * channels] + from_state[channels : 2 * channels]
    )
    state_term = from_state[2 * channels :]
    candidate = jnp.tanh(from_input[2 * channels :] + reset_gate * state_term)
    new_state = ((1.0 - update) * candidate + update * previous.astype(jnp.float32)).astype(
        jnp.bfloat16
    )
    return new_state, (update, reset_gate, candidate, state_term)


def gate_grads(grad_state, saved, previous):
    update, reset_gate, candidate, state_term = saved
    grad_candidate = grad_state * (1.0 - update)
    grad_update = grad_state * (previous.astype(jnp.float32) - candidate)
    pre_update = grad_update * update * (1.0 - update)
    pre_candidate = grad_candidate * (1.0 - candidate * candidate)
    pre_reset = pre_candidate * state_term * reset_gate * (1.0 - reset_gate)
    pre_hidden = pre_candidate * reset_gate
    input_pre = jnp.concatenate([pre_update, pre_reset, pre_candidate], 0).astype(jnp.bfloat16)
    state_pre = jnp.concatenate([pre_update, pre_reset, pre_hidden], 0).astype(jnp.bfloat16)
    return (input_pre, state_pre, grad_state * update)


def reduce_kernel(rows, cols, x_ref, out_ref, got_row, summed, got_col, reduced, gathered, send_sem, recv_sem, own_sem):
    mesh_ids = pl.DeviceIdType.MESH
    me_row, me_col = lax.axis_index("row"), lax.axis_index("col")
    barrier = pltpu.get_barrier_semaphore()
    for axis, me, count in (("row", me_row, rows), ("col", me_col, cols)):

        def greet(distance, carry, axis=axis, me=me, count=count):
            peer = lax.rem(me + distance, count)
            pl.semaphore_signal(barrier, inc=1, device_id={axis: peer}, device_id_type=mesh_ids)
            return carry

        lax.fori_loop(1, count, greet, 0)
    pl.semaphore_wait(barrier, rows + cols - 2)
    piece = summed.shape[0] // cols

    def phase(index, axis, me, count, source, target):
        def copy_to(distance):
            peer = lax.rem(me + distance, count)
            return pltpu.make_async_remote_copy(
                src_ref=source(peer),
                dst_ref=target.at[me],
                send_sem=send_sem.at[index, distance],
                recv_sem=recv_sem.at[index, distance],
                device_id={axis: peer},
                device_id_type=mesh_ids,
            )

        def start(distance, carry):
            copy_to(distance).start()
            return carry

        def finish(distance, carry):
            copy_to(distance).wait()
            return carry

        lax.fori_loop(1, count, start, 0)
        own = pltpu.make_async_copy(source(me), target.at[me], own_sem.at[index])
        own.start()
        own.wait()
        lax.fori_loop(1, count, finish, 0)

    def total_of(buffer, count):
        return lax.fori_loop(1, count, lambda index, acc: acc + buffer[index], buffer[0])

    phase(0, "row", me_row, rows, lambda peer: x_ref.at[peer], got_row)
    summed[...] = total_of(got_row, rows)
    phase(
        1, "col", me_col, cols,
        lambda peer: summed.at[pl.ds(peer * piece, piece)], got_col,
    )
    reduced[...] = total_of(got_col, cols)
    phase(2, "col", me_col, cols, lambda peer: reduced, gathered)
    phase(3, "row", me_row, rows, lambda peer: gathered, out_ref)


def all_sum(parts):
    both = jnp.concatenate(parts, 0)
    rows, cols = lax.axis_size("row"), lax.axis_size("col")
    lanes = 128
    piece = -(-both.size // (rows * cols * lanes))
    chunk = cols * piece * lanes
    padded_size = rows * chunk
    flat = jnp.pad(both.reshape(-1), (0, padded_size - both.size))
    count = max(rows, cols)
    out = pl.pallas_call(
        functools.partial(reduce_kernel, rows, cols),
        out_shape=jax.ShapeDtypeStruct((rows, cols, piece, lanes), jnp.float32),
        in_specs=[pl.BlockSpec(memory_space=pltpu.VMEM)],
        out_specs=pl.BlockSpec(memory_space=pltpu.VMEM),
        scratch_shapes=[
            pltpu.VMEM((rows, cols * piece, lanes), jnp.float32),
            pltpu.VMEM((cols * piece, lanes), jnp.float32),
            pltpu.VMEM((cols, piece, lanes), jnp.float32),
            pltpu.VMEM((piece, lanes), jnp.float32),
            pltpu.VMEM((cols, piece, lanes), jnp.float32),
            pltpu.SemaphoreType.DMA((4, count)),
            pltpu.SemaphoreType.DMA((4, count)),
            pltpu.SemaphoreType.DMA((4,)),
        ],
        compiler_params=pltpu.CompilerParams(collective_id=0, has_side_effects=True),
    )(flat.reshape(rows, cols * piece, lanes))
    return jnp.split(out.reshape(-1)[: both.size].reshape(both.shape), len(parts), 0)


def local(frames, state, input_weight, state_weight, cotangent):
    step_count = frames.shape[0]
    channels = state.shape[0]
    rows, cols = state.shape[1], state.shape[2]
    halo = HALO
    ext_rows, ext_cols = rows + 2 * halo, cols + 2 * halo
    length = ext_rows * ext_cols
    margin = ext_cols + 1
    offsets = [(k // 3 - 1) * ext_cols + (k % 3 - 1) for k in range(9)]

    fields = jnp.concatenate([frames.reshape(-1, rows, cols), state, cotangent], 0)
    fields = padded_2(fields, (("row", 1), ("col", 2)), halo).reshape(-1, length)
    frame_flat = [fields[t * frames.shape[1] : (t + 1) * frames.shape[1]] for t in range(step_count)]
    base = step_count * frames.shape[1]
    state_flat = fields[base : base + channels]
    cot_flat = fields[base + channels :]

    r = lax.broadcasted_iota(jnp.int32, (ext_rows, ext_cols), 0)
    c = lax.broadcasted_iota(jnp.int32, (ext_rows, ext_cols), 1)
    global_r = lax.axis_index("row") * rows + r - halo
    global_c = lax.axis_index("col") * cols + c - halo
    inside = (
        (global_r >= 0)
        & (global_r < rows * lax.axis_size("row"))
        & (global_c >= 0)
        & (global_c < cols * lax.axis_size("col"))
    ).reshape(1, length)
    own = ((r >= halo) & (r < halo + rows) & (c >= halo) & (c < halo + cols)).reshape(1, length)

    def pad(flat):
        return jnp.pad(flat, ((0, 0), (margin, margin)))

    records = []
    current = state_flat
    for step_index in range(step_count):
        frame_pad, state_pad = pad(frame_flat[step_index]), pad(current)
        from_input = conv_flat(input_weight, frame_pad, offsets, margin, length)
        from_state = conv_flat(state_weight, state_pad, offsets, margin, length)
        new_state, saved = gates(from_input, from_state, current, channels)
        records.append((frame_pad, state_pad, current, saved))
        current = jnp.where(inside, new_state, jnp.zeros_like(new_state))

    grad_state = cot_flat.astype(jnp.float32)
    input_pres, input_fields, state_pres, state_fields = [], [], [], []
    for step_index in reversed(range(step_count)):
        frame_pad, state_pad, previous, saved = records[step_index]
        input_pre, state_pre, direct = gate_grads(grad_state, saved, previous)
        input_pres.append(jnp.where(own, input_pre, jnp.zeros_like(input_pre)))
        state_pres.append(jnp.where(own, state_pre, jnp.zeros_like(state_pre)))
        input_fields.append(frame_pad)
        state_fields.append(state_pad)
        state_pre = jnp.where(inside, state_pre, jnp.zeros_like(state_pre))
        grad_state = direct + spread_flat(state_weight, pad(state_pre), offsets, margin, length)

    input_sum = sum(
        weight_flat(p, f, offsets, margin, length) for p, f in zip(input_pres, input_fields)
    )
    state_sum = sum(
        weight_flat(p, f, offsets, margin, length) for p, f in zip(state_pres, state_fields)
    )
    input_sum, state_sum = all_sum([input_sum, state_sum])
    taps, out_ch, in_ch = input_weight.shape
    input_sum = input_sum.reshape(out_ch, taps, in_ch).transpose(1, 0, 2)
    taps, out_ch, in_ch = state_weight.shape
    state_sum = state_sum.reshape(out_ch, taps, in_ch).transpose(1, 0, 2)
    loss_scale = (rows * lax.axis_size("row") * cols * lax.axis_size("col")) ** (-0.5)

    def crop(flat):
        return flat.reshape(-1, ext_rows, ext_cols)[:, halo : halo + rows, halo : halo + cols]

    return (crop(current), crop(grad_state), input_sum * loss_scale, state_sum * loss_scale)


def solution(mesh):
    in_specs = (P(None, None, "row", "col"), P(None, "row", "col"), P(), P(), P(None, "row", "col"))
    out_specs = (P(None, "row", "col"), P(None, "row", "col"), P(), P())
    return jax.shard_map(local, mesh=mesh, in_specs=in_specs, out_specs=out_specs, check_vma=False)
```
